512 devices in a mesh: span: 8 (over z), chord: 8 (over x, y_lo), normal: 8 (over y_hi, core).
Axes of the slice: x: 4, y: 8 (y_hi: 4, y_lo: 2; y = y_hi * 2 + y_lo), z: 8, core: 2. Of those that a mesh axis runs over, the one named last changes fastest.
Arguments:
- state: float32 [5, 128, 64, 1024], P(None, 'chord', 'normal', 'span'), may hold values from -0.5 to 5
- metrics: float32 [9, 128, 64, 1024], P(None, 'chord', 'normal', 'span'), may hold values from -1 to 1
- face_codes: int32 [8, 8, 8, 6], P('chord', 'normal', 'span'), may hold values from 0 to 4, as said below
- inverse_i: float32 [8, 8, 8, 16, 16], P('chord', 'normal', 'span'), may hold values from -1 to 1
- inverse_j: float32 [8, 8, 8, 8, 8], P('chord', 'normal', 'span'), may hold values from -1 to 1
- inverse_k: float32 [8, 8, 8, 128, 128], P('chord', 'normal', 'span'), may hold values from -1 to 1
Outputs:
- increment: float32 [5, 128, 64, 1024], P(None, 'chord', 'normal', 'span')
The draws below stay inside these ranges and needn't reach their ends.
Inputs may be any that keep to these rules, and one draw needn't show every extreme that they name: `face_codes`: for each block, the codes of its lower and upper chordwise faces, lower and upper wall-normal faces, lower and upper spanwise faces, in that order: 0 for a boundary face, else 1 plus two orientation bits; a face and the facing face of its neighbour block along that direction carry the same code.
All inputs are finite; a program needn't handle non-finite values.
Results may differ from the reference program's by a relative error of at most 0.0001.
Values sent between devices are 32-bit elements; how exact they have to be, the bound alone decides.
A program may use at most 64 MiB of HBM per device.

```python
import jax
import jax.numpy as jnp
from jax import lax

CI = 16
CJ = 8
CK = 128
METRICS = 9
ITERS = 2
BLK_I = 8
BLK_J = 8
BLK_K = 8
NI = 128
NJ = 64
NK = 1024


def draw_state(key, part):
    base = jax.random.fold_in(key, 21)
    keys = jax.random.split(base, 3)
    shape = (NI, NJ, NK)
    first = jax.random.uniform(keys[0], shape, jnp.float32)
    second = jax.random.uniform(keys[1], (3,) + shape, jnp.float32)
    third = jax.random.uniform(keys[2], shape, jnp.float32)
    density = 1.0 + first
    momentum = second - 0.5
    energy = 3.0 + 2.0 * third
    return jnp.concatenate([density[None], momentum, energy[None]], axis=0).astype(jnp.float32)


def draw_face_codes(key, part):
    base = jax.random.fold_in(key, 31)
    keys = jax.random.split(base, 3)
    shape = (BLK_I, BLK_J, BLK_K)
    upper_i = jax.random.randint(keys[0], shape, 0, 5)
    upper_j = jax.random.randint(keys[1], shape, 0, 5)
    upper_k = jax.random.randint(keys[2], shape, 0, 5)
    lower_i = jnp.roll(upper_i, 1, axis=0)
    lower_j = jnp.roll(upper_j, 1, axis=1)
    lower_k = jnp.roll(upper_k, 1, axis=2)
    return jnp.stack([lower_i, upper_i, lower_j, upper_j, lower_k, upper_k], axis=-1).astype(jnp.int32)


def line_inverse(key, extent):
    keys = jax.random.split(key, 2)
    shape = (BLK_I, BLK_J, BLK_K, extent, extent)
    diagonal = jax.random.uniform(keys[0], shape[:-1], jnp.float32, 0.3, 0.6)
    spread = jax.random.uniform(keys[1], shape, jnp.float32, -1.0, 1.0)
    identity = jnp.eye(extent, dtype=jnp.float32)
    return (spread * (0.4 / extent) * (1.0 - identity) + diagonal[..., None] * identity).astype(jnp.float32)


def draw_inverse_i(key, part):
    return line_inverse(jax.random.fold_in(key, 11), CI)


def draw_inverse_j(key, part):
    return line_inverse(jax.random.fold_in(key, 12), CJ)


def draw_inverse_k(key, part):
    return line_inverse(jax.random.fold_in(key, 13), CK)


def block_levels(rng, shape, cuts, smallest, top_value):
    def one(dim, shards_of):
        steps = jax.random.uniform(jax.random.fold_in(jax.random.fold_in(rng, 6), dim), (shards_of,), jnp.float32, smallest / len(cuts), top_value / len(cuts))
        return jnp.repeat(jnp.exp(steps), shape[dim] // shards_of).reshape((-1,) + (1,) * (len(shape) - dim - 1))

    level = one(*cuts[0])
    for cut in cuts[1:]:
        level = level * one(*cut)
    return level


def setup_inputs(seed: int = 0) -> dict:
    seeds = jax.random.split(jax.random.key(seed), 7)
    state = draw_state(jax.random.fold_in(seeds[6], 71), 0)
    metrics = jnp.clip(jax.random.uniform(seeds[1], (METRICS, NI, NJ, NK), jnp.float32, -1.0, 1.0) * block_levels(seeds[1], (METRICS, NI, NJ, NK), ((1, 8), (2, 8), (3, 8)), -0.4, 0.0), -1.0, 1.0)
    face_codes = draw_face_codes(jax.random.fold_in(seeds[6], 71), 0)
    inverse_i = draw_inverse_i(jax.random.fold_in(seeds[6], 71), 0)
    inverse_j = draw_inverse_j(jax.random.fold_in(seeds[6], 71), 0)
    inverse_k = draw_inverse_k(jax.random.fold_in(seeds[6], 71), 0)
    return {"state": state, "metrics": metrics, "face_codes": face_codes, "inverse_i": inverse_i, "inverse_j": inverse_j, "inverse_k": inverse_k}


gas_factor = 0.4
damping = 0.1
pseudo_step = 0.03


def orient(slab, code_full, axes_in):
    for power, axis_in in enumerate(axes_in):
        flag = jnp.logical_and(code_full > 0, ((code_full - 1) // (2 ** power)) % 2 == 1)
        slab = jnp.where(flag, jnp.flip(slab, axis=axis_in), slab)
    return slab


def ghosted(block_full, codes, direction, width):
    axis_block = 1 + 2 * direction
    axis_cell = 2 + 2 * direction
    length = block_full.shape[axis_cell]
    lower = lax.slice_in_dim(block_full, 0, width, axis=axis_cell)
    upper = lax.slice_in_dim(block_full, length - width, length, axis=axis_cell)
    from_above = jnp.roll(lower, -1, axis=axis_block)
    from_below = jnp.roll(upper, 1, axis=axis_block)
    axes_in = [2 + 2 * other for other in range(3) if other != direction]
    code_low = codes[:, :, :, 2 * direction][None, :, None, :, None, :, None]
    code_high = codes[:, :, :, 2 * direction + 1][None, :, None, :, None, :, None]
    ghost_low = jnp.where(code_low > 0, orient(from_below, code_low, axes_in), jnp.flip(lower, axis=axis_cell))
    ghost_high = jnp.where(code_high > 0, orient(from_above, code_high, axes_in), jnp.flip(upper, axis=axis_cell))
    return jnp.concatenate([ghost_low, block_full, ghost_high], axis=axis_cell)


def flux_of(fields, triple):
    density = fields[0]
    mom_x = fields[1]
    mom_y = fields[2]
    mom_z = fields[3]
    energy = fields[4]
    kinetic = 0.5 * (mom_x * mom_x + mom_y * mom_y + mom_z * mom_z) / density
    pressure = gas_factor * (energy - kinetic)
    speed = (triple[0] * mom_x + triple[1] * mom_y + triple[2] * mom_z) / density
    return jnp.stack([density * speed, mom_x * speed + triple[0] * pressure,
                      mom_y * speed + triple[1] * pressure, mom_z * speed + triple[2] * pressure,
                      (energy + pressure) * speed])


def residual(state_full, metric_full, codes):
    total = jnp.zeros(state_full.shape, jnp.float32)
    for direction in range(3):
        axis_cell = 2 + 2 * direction
        length = state_full.shape[axis_cell]
        fields = ghosted(state_full, codes, direction, 2)
        triple = ghosted(metric_full[3 * direction:3 * direction + 3], codes, direction, 1)
        inner = lax.slice_in_dim(fields, 1, length + 3, axis=axis_cell)
        fluxes = flux_of(inner, triple)
        central = 0.5 * (lax.slice_in_dim(fluxes, 2, length + 2, axis=axis_cell)
                         - lax.slice_in_dim(fluxes, 0, length, axis=axis_cell))
        parts = [lax.slice_in_dim(fields, offset, offset + length, axis=axis_cell) for offset in range(5)]
        fourth = parts[0] - 4.0 * parts[1] + 6.0 * parts[2] - 4.0 * parts[3] + parts[4]
        total = total - central - damping * fourth
    return total


def line_solve(values, inverse_i, inverse_j, inverse_k):
    highest = lax.Precision.HIGHEST
    values = jnp.einsum('fbicjdk,bcdlk->fbicjdl', values, inverse_k, precision=highest)
    values = jnp.einsum('fbicjdk,bcdlj->fbicldk', values, inverse_j, precision=highest)
    return jnp.einsum('fbicjdk,bcdli->fblcjdk', values, inverse_i, precision=highest)


def reference(state, metrics, face_codes, inverse_i, inverse_j, inverse_k):
    blocks_i, blocks_j, blocks_k = face_codes.shape[0], face_codes.shape[1], face_codes.shape[2]
    cells_i = inverse_i.shape[3]
    cells_j = inverse_j.shape[3]
    cells_k = inverse_k.shape[3]
    full_shape = (blocks_i, cells_i, blocks_j, cells_j, blocks_k, cells_k)
    current = state.reshape((state.shape[0],) + full_shape)
    metric_full = metrics.reshape((metrics.shape[0],) + full_shape)
    total = jnp.zeros(current.shape, jnp.float32)
    for sweep in range(ITERS):
        change = line_solve(residual(current, metric_full, face_codes), inverse_i, inverse_j, inverse_k)
        total = total + change
        current = current + pseudo_step * change
    return total.reshape(state.shape)
```

```python
import functools

import jax
import jax.numpy as jnp
from jax import lax
from jax.experimental import pallas as pl
from jax.experimental.pallas import tpu as pltpu
from jax.sharding import PartitionSpec as P

MESH = pl.DeviceIdType.MESH
HIGHEST = lax.Precision.HIGHEST
AXES = ("chord", "normal", "span")
SWEEPS = 2
FIELDS = 5
NI, NJ, NK = 16, 8, 128
CELLS = NI * NJ

gas_factor = 0.4
damping = 0.1
pseudo_step = 0.03


def dot(a, b, contract):
    return lax.dot_general(
        a, b, (contract, ((), ())), precision=HIGHEST, preferred_element_type=jnp.float32
    )


def thermo(g):
    inv = 1.0 / g[0]
    kinetic = 0.5 * (g[1] * g[1] + g[2] * g[2] + g[3] * g[3]) * inv
    pressure = gas_factor * (g[4] - kinetic)
    return inv, pressure


def flux(g, inv, pressure, n):
    speed = (n[0] * g[1] + n[1] * g[2] + n[2] * g[3]) * inv
    return [
        g[0] * speed,
        g[1] * speed + n[0] * pressure,
        g[2] * speed + n[1] * pressure,
        g[3] * speed + n[2] * pressure,
        (g[4] + pressure) * speed,
    ]


def face_terms(edge, behind, n, half):
    inv, pressure = thermo(edge)
    f = flux(edge, inv, pressure, n)
    send, keep, far = [], [], []
    for v in range(FIELDS):
        smooth = 4.0 * damping * edge[v] - damping * behind[v]
        send.append(smooth + half * f[v])
        keep.append(smooth - half * f[v])
        far.append(-damping * edge[v])
    return send, keep, far


def lanes(x, index):
    return jnp.take_along_axis(x, index, axis=1, mode="promise_in_bounds")


def rows(x, index):
    return jnp.take_along_axis(x, index, axis=0, mode="promise_in_bounds")


def kernel(
    codes, state, metrics, inv_i, inv_j, inv_k, out,
    u, n, r, gi, t, m_ij, n_k,
    send_i, send_j, send_k, keep_i, keep_j, keep_k, recv_i, recv_j, recv_k,
    load_sem, send_sem, recv_sem,
):
    load_u = pltpu.make_async_copy(state, u.at[:, pl.ds(2 * NJ, CELLS), :], load_sem.at[0])
    load_n = pltpu.make_async_copy(metrics, n, load_sem.at[1])
    load_u.start()
    load_n.start()

    near = []
    for axis in AXES:
        size, me = lax.axis_size(axis), lax.axis_index(axis)
        near.append((lax.rem(me + size - 1, size), lax.rem(me + 1, size)))
    barrier = pltpu.get_barrier_semaphore()
    for d, axis in enumerate(AXES):
        for side in range(2):
            pl.semaphore_signal(
                barrier, inc=1, device_id={axis: near[d][side]}, device_id_type=MESH
            )

    sends = (send_i, send_j, send_k)
    recvs = (recv_i, recv_j, recv_k)

    def copy(sweep, d, side):
        return pltpu.make_async_remote_copy(
            src_ref=sends[d].at[sweep, side],
            dst_ref=recvs[d].at[sweep, 1 - side],
            send_sem=send_sem.at[sweep, d, side],
            recv_sem=recv_sem.at[sweep, d, 1 - side],
            device_id={AXES[d]: near[d][side]},
            device_id_type=MESH,
        )

    copies = [[[copy(s, d, side) for side in range(2)] for d in range(3)] for s in range(SWEEPS)]

    sub = lax.broadcasted_iota(jnp.int32, (8, NK), 0)
    lane = lax.broadcasted_iota(jnp.int32, (8, NK), 1)
    low4 = jnp.bitwise_and(sub, 3)
    picked = jnp.where(
        low4 == 0, 0, jnp.where(low4 == 1, NK - 1, jnp.where(low4 == 2, 1, NK - 2))
    )
    pick = jnp.where(lane == picked, 1.0, 0.0).astype(jnp.float32)
    place = jnp.where(sub < 4, pick, 0.0)
    even = jnp.bitwise_and(sub, 1) == 0
    lane_rev = NK - 1 - lane
    row_rev = 7 - sub
    lane_rev_i = jnp.bitwise_xor(lane, CELLS - NJ)
    lane_rev_j = jnp.bitwise_xor(lane, NJ - 1)

    code = [jnp.full((8, NK), codes[0, q], jnp.int32) for q in range(6)]
    bit0 = [jnp.bitwise_and(c - 1, 1) == 1 for c in code]
    bit1 = [jnp.bitwise_and(c - 1, 2) == 2 for c in code]
    joined = [c > 0 for c in code]

    zero = jnp.zeros((2 * NJ, NK), jnp.float32)
    for v in range(FIELDS):
        u[v, pl.ds(0, 2 * NJ), :] = zero
        u[v, pl.ds(2 * NJ + CELLS, 2 * NJ), :] = zero
        gi[v, pl.ds(0, NJ), :] = zero[:NJ]
        gi[v, pl.ds(NJ + CELLS, NJ), :] = zero[:NJ]

    load_u.wait()
    load_n.wait()

    def edge_i(sweep):
        for side in range(2):
            at = 0 if side == 0 else NI - 1
            back = 1 if side == 0 else NI - 2
            edge = [u[v, pl.ds((2 + at) * NJ, NJ), :] for v in range(FIELDS)]
            behind = [u[v, pl.ds((2 + back) * NJ, NJ), :] for v in range(FIELDS)]
            nn = [n[c, pl.ds(at * NJ, NJ), :] for c in range(3)]
            send, keep, far = face_terms(edge, behind, nn, -0.5 if side == 0 else 0.5)
            for v in range(FIELDS):
                send_i[sweep, side, v] = send[v]
                send_i[sweep, side, FIELDS + v] = far[v]
                keep_i[side, v] = keep[v]

    def edge_j(sweep):
        for side in range(2):
            at = 0 if side == 0 else NJ - 1
            back = 1 if side == 0 else NJ - 2
            edge = [u[v, pl.ds(2 * NJ + at, NI, stride=NJ), :] for v in range(FIELDS)]
            behind = [u[v, pl.ds(2 * NJ + back, NI, stride=NJ), :] for v in range(FIELDS)]
            nn = [n[3 + c, pl.ds(at, NI, stride=NJ), :] for c in range(3)]
            send, keep, far = face_terms(edge, behind, nn, -0.5 if side == 0 else 0.5)
            for v in range(FIELDS):
                send_j[sweep, side, v] = send[v]
                send_j[sweep, side, FIELDS + v] = far[v]
                keep_j[side, v] = keep[v]

    def edge_k(sweep):
        edge = [dot(pick, u[v, pl.ds(2 * NJ, CELLS), :], ((1,), (1,))) for v in range(FIELDS)]
        behind = [pltpu.roll(e, 6, 0) for e in edge]
        nn = [n_k[c] for c in range(3)]
        half = jnp.where(even, -0.5, 0.5)
        send, keep, far = face_terms(edge, behind, nn, half)
        for v in range(FIELDS):
            far_rows = pltpu.roll(far[v], 2, 0)
            send_k[sweep, 0, v] = jnp.where(sub < 2, send[v], far_rows)
            send_k[sweep, 1, v] = jnp.where(sub < 2, send[v], far_rows)
            keep_k[v] = jnp.where(sub < 2, keep[v], far_rows)

    def interior():
        first_j, last_j = sub == 0, sub == NJ - 1
        first_k, last_k = lane == 0, lane == NK - 1

        def slab(i, carry):
            at = pl.multiple_of(i * NJ, NJ)
            g = [u[v, pl.ds(2 * NJ + at, NJ), :] for v in range(FIELDS)]
            nn = [n[c, pl.ds(at, NJ), :] for c in range(9)]
            inv, pressure = thermo(g)
            f = flux(g, inv, pressure, nn[0:3])
            for v in range(FIELDS):
                gi[v, pl.ds(NJ + at, NJ), :] = 0.5 * f[v]
            total = [-18.0 * damping * g[v] for v in range(FIELDS)]
            for d, axis, length, first, last in (
                (1, 0, NJ, first_j, last_j), (2, 1, NK, first_k, last_k),
            ):
                f = flux(g, inv, pressure, nn[3 * d : 3 * d + 3])
                for v in range(FIELDS):
                    def above(x):
                        return jnp.where(last, 0.0, pltpu.roll(x, length - 1, axis))

                    def below(x):
                        return jnp.where(first, 0.0, pltpu.roll(x, 1, axis))

                    smooth, half = 4.0 * damping * g[v], 0.5 * f[v]
                    up = smooth - half - damping * above(g[v])
                    down = smooth + half - damping * below(g[v])
                    total[v] = total[v] + above(up) + below(down)
            for v in range(FIELDS):
                r[v, pl.ds(at, NJ), :] = total[v]
            return carry

        lax.fori_loop(0, NI, slab, 0)

        def chord(i, carry):
            at = pl.multiple_of(i * NJ, NJ)
            for v in range(FIELDS):
                layer = [u[v, pl.ds(at + q * NJ, NJ), :] for q in (0, 1, 3, 4)]
                r[v, pl.ds(at, NJ), :] = (
                    r[v, pl.ds(at, NJ), :]
                    + gi[v, pl.ds(at, NJ), :]
                    - gi[v, pl.ds(at + 2 * NJ, NJ), :]
                    + 4.0 * damping * (layer[1] + layer[2])
                    - damping * (layer[0] + layer[3])
                )
            return carry

        lax.fori_loop(0, NI, chord, 0)

    def halo_k(sweep):
        for side in range(2):
            copies[sweep][2][1 - side].wait_recv()
        lo, hi = 4, 5
        flip_i = jnp.where(even, bit0[lo].astype(jnp.int32), bit0[hi].astype(jnp.int32)) == 1
        flip_j = jnp.where(even, bit1[lo].astype(jnp.int32), bit1[hi].astype(jnp.int32)) == 1
        linked = jnp.where(even, code[lo], code[hi]) > 0
        for v in range(FIELDS):
            z = jnp.where(
                even, pltpu.roll(recv_k[sweep, 0, v], 7, 0), pltpu.roll(recv_k[sweep, 1, v], 1, 0)
            )
            z = jnp.where(flip_i, lanes(z, lane_rev_i), z)
            z = jnp.where(flip_j, lanes(z, lane_rev_j), z)
            z = jnp.where(linked, z, keep_k[v])
            r[v] = r[v] + dot(z, place, ((0,), (0,)))

    def halo_i(sweep):
        for side in range(2):
            copies[sweep][0][1 - side].wait_recv()
            face = side
            for q in range(2 * FIELDS):
                v = q % FIELDS
                x = recv_i[sweep, side, q]
                x = jnp.where(bit0[face], rows(x, row_rev), x)
                x = jnp.where(bit1[face], lanes(x, lane_rev), x)
                own = keep_i[side, v] if q < FIELDS else send_i[sweep, side, q]
                x = jnp.where(joined[face], x, own)
                depth = 0 if q < FIELDS else 1
                at = (depth if side == 0 else NI - 1 - depth) * NJ
                r[v, pl.ds(at, NJ), :] = r[v, pl.ds(at, NJ), :] + x

    def halo_j(sweep):
        for side in range(2):
            copies[sweep][1][1 - side].wait_recv()
            face = 2 + side
            for q in range(2 * FIELDS):
                v = q % FIELDS
                x = [recv_j[sweep, side, q, pl.ds(8 * h, 8), :] for h in range(2)]
                rev = [rows(x[1 - h], row_rev) for h in range(2)]
                x = [jnp.where(bit0[face], rev[h], x[h]) for h in range(2)]
                x = [jnp.where(bit1[face], lanes(x[h], lane_rev), x[h]) for h in range(2)]
                depth = 0 if q < FIELDS else 1
                at = depth if side == 0 else NJ - 1 - depth
                for h in range(2):
                    part = pl.ds(8 * h, 8)
                    own = keep_j[side, v, part, :] if q < FIELDS else send_j[sweep, side, q, part, :]
                    y = jnp.where(joined[face], x[h], own)
                    where = pl.ds(8 * h * NJ + at, 8, stride=NJ)
                    r[v, where, :] = r[v, where, :] + y

    def solve(sweep):
        for v in range(FIELDS):
            t[v] = dot(r[v], inv_k[...], ((1,), (1,)))
        for v in range(FIELDS):
            change = dot(m_ij[...], t[v], ((1,), (0,)))
            if sweep == 0:
                out[v] = change
                inner = pl.ds(2 * NJ, CELLS)
                u[v, inner, :] = u[v, inner, :] + pseudo_step * change
            else:
                out[v] = out[v] + change

    for sweep in range(SWEEPS):
        edge_j(sweep)
        if sweep == 0:
            pl.semaphore_wait(barrier, 6)
        for side in range(2):
            copies[sweep][1][side].start()
        edge_i(sweep)
        for side in range(2):
            copies[sweep][0][side].start()
        if sweep == 0:
            for c in range(3):
                n_k[c] = dot(pick, n[6 + c], ((1,), (1,)))
        edge_k(sweep)
        for side in range(2):
            copies[sweep][2][side].start()
        interior()
        if sweep == 0:
            wide = lax.broadcasted_iota(jnp.int32, (CELLS, NI), 0)
            e_i = jnp.where(
                lax.shift_right_logical(wide, 3)
                == lax.broadcasted_iota(jnp.int32, (CELLS, NI), 1), 1.0, 0.0,
            ).astype(jnp.float32)
            wide = lax.broadcasted_iota(jnp.int32, (CELLS, NJ), 0)
            e_j = jnp.where(
                jnp.bitwise_and(wide, 7) == lax.broadcasted_iota(jnp.int32, (CELLS, NJ), 1), 1.0, 0.0
            ).astype(jnp.float32)
            big_i = dot(dot(e_i, inv_i[...], ((1,), (0,))), e_i, ((1,), (1,)))
            big_j = dot(dot(e_j, inv_j[...], ((1,), (0,))), e_j, ((1,), (1,)))
            m_ij[...] = big_i * big_j
        halo_k(sweep)
        halo_i(sweep)
        halo_j(sweep)
        solve(sweep)

    for sweep in range(SWEEPS):
        for d in range(3):
            for side in range(2):
                copies[sweep][d][side].wait_send()


def local(state, metrics, face_codes, inverse_i, inverse_j, inverse_k):
    f32 = jnp.float32
    vmem = pl.BlockSpec(memory_space=pltpu.VMEM)
    anywhere = pl.BlockSpec(memory_space=pl.ANY)
    result = pl.pallas_call(
        kernel,
        out_shape=jax.ShapeDtypeStruct((FIELDS, CELLS, NK), f32),
        in_specs=[pl.BlockSpec(memory_space=pltpu.SMEM), anywhere, anywhere, vmem, vmem, vmem],
        out_specs=vmem,
        scratch_shapes=[
            pltpu.VMEM((FIELDS, CELLS + 4 * NJ, NK), f32),
            pltpu.VMEM((9, CELLS, NK), f32),
            pltpu.VMEM((FIELDS, CELLS, NK), f32),
            pltpu.VMEM((FIELDS, CELLS + 2 * NJ, NK), f32),
            pltpu.VMEM((FIELDS, CELLS, NK), f32),
            pltpu.VMEM((CELLS, CELLS), f32),
            pltpu.VMEM((3, 8, NK), f32),
            pltpu.VMEM((SWEEPS, 2, 2 * FIELDS, NJ, NK), f32),
            pltpu.VMEM((SWEEPS, 2, 2 * FIELDS, NI, NK), f32),
            pltpu.VMEM((SWEEPS, 2, FIELDS, 8, NK), f32),
            pltpu.VMEM((2, FIELDS, NJ, NK), f32),
            pltpu.VMEM((2, FIELDS, NI, NK), f32),
            pltpu.VMEM((FIELDS, 8, NK), f32),
            pltpu.VMEM((SWEEPS, 2, 2 * FIELDS, NJ, NK), f32),
            pltpu.VMEM((SWEEPS, 2, 2 * FIELDS, NI, NK), f32),
            pltpu.VMEM((SWEEPS, 2, FIELDS, 8, NK), f32),
            pltpu.SemaphoreType.DMA((2,)),
            pltpu.SemaphoreType.DMA((SWEEPS, 3, 2)),
            pltpu.SemaphoreType.DMA((SWEEPS, 3, 2)),
        ],
        compiler_params=pltpu.CompilerParams(collective_id=0, has_side_effects=True),
        name="adi",
    )(
        face_codes.reshape(1, 6),
        state.reshape(FIELDS, CELLS, NK),
        metrics.reshape(9, CELLS, NK),
        inverse_i.reshape(NI, NI),
        inverse_j.reshape(NJ, NJ),
        inverse_k.reshape(NK, NK),
    )
    return result.reshape(state.shape)


def solution(mesh):
    cells = P(None, "chord", "normal", "span")
    block = P("chord", "normal", "span", None, None)
    return jax.shard_map(
        local,
        mesh=mesh,
        in_specs=(cells, cells, P("chord", "normal", "span", None), block, block, block),
        out_specs=cells,
        check_vma=False,
    )
```

```python
import functools

import jax
import jax.numpy as jnp
from jax import lax
from jax.experimental import pallas as pl
from jax.experimental.pallas import tpu as pltpu
from jax.sharding import PartitionSpec as P

MESH = pl.DeviceIdType.MESH
HIGHEST = lax.Precision.HIGHEST
BF16 = jnp.bfloat16
AXES = ("chord", "normal", "span")
SWEEPS = 2
FIELDS = 5
NI, NJ, NK = 16, 8, 128
CELLS = NI * NJ

gas_factor = 0.4
damping = 0.1
pseudo_step = 0.03


def dot(a, b, contract):
    return lax.dot_general(
        a, b, (contract, ((), ())), precision=HIGHEST, preferred_element_type=jnp.float32
    )


def thermo(g):
    inv = 1.0 / g[0]
    kinetic = 0.5 * (g[1] * g[1] + g[2] * g[2] + g[3] * g[3]) * inv
    pressure = gas_factor * (g[4] - kinetic)
    return inv, pressure


def flux(g, inv, pressure, n):
    speed = (n[0] * g[1] + n[1] * g[2] + n[2] * g[3]) * inv
    return [
        g[0] * speed,
        g[1] * speed + n[0] * pressure,
        g[2] * speed + n[1] * pressure,
        g[3] * speed + n[2] * pressure,
        (g[4] + pressure) * speed,
    ]


def face_terms(edge, behind, n, half):
    inv, pressure = thermo(edge)
    f = flux(edge, inv, pressure, n)
    send, keep, far = [], [], []
    for v in range(FIELDS):
        smooth = 4.0 * damping * edge[v] - damping * behind[v]
        send.append(smooth + half * f[v])
        keep.append(smooth - half * f[v])
        far.append(-damping * edge[v])
    return send, keep, far


def halves(x):
    high = x.astype(BF16)
    return high, (x - high.astype(jnp.float32)).astype(BF16)


def product(a, b):
    both = lax.dot_general(
        a, b, (((1,), (0,)), ((), ())), preferred_element_type=jnp.float32
    )
    return both[:, :NK] + both[:, NK:]


def lanes(x, index):
    return jnp.take_along_axis(x, index, axis=1, mode="promise_in_bounds")


def rows(x, index):
    return jnp.take_along_axis(x, index, axis=0, mode="promise_in_bounds")


def kernel(
    codes_hbm, state, metrics, inv_i_hbm, inv_j_hbm, inv_k_hbm, out,
    codes, u, n, inv_i, inv_j, inv_k, r, gi, r2, w_k, m2, cross, n_k,
    send_i, send_j, send_k, keep_i, keep_j, keep_k, recv_i, recv_j, recv_k,
    load_sem, send_sem, recv_sem,
):
    load_u = pltpu.make_async_copy(state, u.at[:, pl.ds(2 * NJ, CELLS), :], load_sem.at[0])
    load_n = pltpu.make_async_copy(metrics, n, load_sem.at[1])
    load_rest = [
        pltpu.make_async_copy(a, b, load_sem.at[2 + q])
        for q, (a, b) in enumerate((
            (codes_hbm, codes), (inv_i_hbm, inv_i), (inv_j_hbm, inv_j), (inv_k_hbm, inv_k),
        ))
    ]
    load_u.start()
    load_n.start()
    for load in load_rest:
        load.start()

    near = []
    for axis in AXES:
        size, me = lax.axis_size(axis), lax.axis_index(axis)
        near.append((lax.rem(me + size - 1, size), lax.rem(me + 1, size)))
    barrier = pltpu.get_barrier_semaphore()
    for d, axis in enumerate(AXES):
        for side in range(2):
            pl.semaphore_signal(
                barrier, inc=1, device_id={axis: near[d][side]}, device_id_type=MESH
            )

    sends = (send_i, send_j, send_k)
    recvs = (recv_i, recv_j, recv_k)

    def copy(sweep, d, side):
        return pltpu.make_async_remote_copy(
            src_ref=sends[d].at[sweep] if d == 2 else sends[d].at[sweep, side],
            dst_ref=recvs[d].at[sweep, 1 - side],
            send_sem=send_sem.at[sweep, d, side],
            recv_sem=recv_sem.at[sweep, d, 1 - side],
            device_id={AXES[d]: near[d][side]},
            device_id_type=MESH,
        )

    copies = [[[copy(s, d, side) for side in range(2)] for d in range(3)] for s in range(SWEEPS)]

    sub = lax.broadcasted_iota(jnp.int32, (8, NK), 0)
    lane = lax.broadcasted_iota(jnp.int32, (8, NK), 1)
    lane_rev = NK - 1 - lane
    row_rev = 7 - sub
    row_swap = jnp.where(sub < 4, 3 - sub, sub)
    outer_k = jnp.logical_or(sub == 1, sub == 2)
    top_k = sub < 2
    last_k4 = jnp.logical_or(lane < 2, lane >= NK - 2)
    lane_rev_i = jnp.bitwise_xor(lane, CELLS - NJ)
    lane_rev_j = jnp.bitwise_xor(lane, NJ - 1)

    def read_codes():
        code = [jnp.full((8, NK), codes[0, q], jnp.int32) for q in range(6)]
        bit0 = [jnp.bitwise_and(c - 1, 1) == 1 for c in code]
        bit1 = [jnp.bitwise_and(c - 1, 2) == 2 for c in code]
        joined = [c > 0 for c in code]
        return code, bit0, bit1, joined

    zero = jnp.zeros((2 * NJ, NK), jnp.float32)
    for v in range(FIELDS):
        u[v, pl.ds(0, 2 * NJ), :] = zero
        u[v, pl.ds(2 * NJ + CELLS, 2 * NJ), :] = zero
        gi[v, pl.ds(0, NJ), :] = zero[:NJ]
        gi[v, pl.ds(NJ + CELLS, NJ), :] = zero[:NJ]
    cross[...] = jnp.zeros((CELLS, NK), jnp.float32)

    load_u.wait()
    load_n.wait()

    def edge_i(sweep):
        for side in range(2):
            at = 0 if side == 0 else NI - 1
            back = 1 if side == 0 else NI - 2
            edge = [u[v, pl.ds((2 + at) * NJ, NJ), :] for v in range(FIELDS)]
            behind = [u[v, pl.ds((2 + back) * NJ, NJ), :] for v in range(FIELDS)]
            nn = [n[c, pl.ds(at * NJ, NJ), :] for c in range(3)]
            send, keep, far = face_terms(edge, behind, nn, -0.5 if side == 0 else 0.5)
            for v in range(FIELDS):
                send_i[sweep, side, v] = send[v]
                send_i[sweep, side, FIELDS + v] = far[v]
                keep_i[side, v] = keep[v]

    def edge_j(sweep):
        for side in range(2):
            at = 0 if side == 0 else NJ - 1
            back = 1 if side == 0 else NJ - 2
            edge = [u[v, pl.ds(2 * NJ + at, NI, stride=NJ), :] for v in range(FIELDS)]
            behind = [u[v, pl.ds(2 * NJ + back, NI, stride=NJ), :] for v in range(FIELDS)]
            nn = [n[3 + c, pl.ds(at, NI, stride=NJ), :] for c in range(3)]
            send, keep, far = face_terms(edge, behind, nn, -0.5 if side == 0 else 0.5)
            for v in range(FIELDS):
                send_j[sweep, side, v] = send[v]
                send_j[sweep, side, FIELDS + v] = far[v]
                keep_j[side, v] = keep[v]

    def edge_k(sweep):
        for i in range(NI):
            x = [u[v, pl.ds((2 + i) * NJ, NJ), :] for v in range(FIELDS)]
            if sweep == 0:
                x = x + [n[6 + c, pl.ds(i * NJ, NJ), :] for c in range(3)]
            y = pltpu.roll(x[0], 2, 1)
            for v in range(1, len(x)):
                y = jnp.where(lane >= 8 * v, pltpu.roll(x[v], 8 * v + 2, 1), y)
            cross[pl.ds(i * NJ, NJ), :] = y
        packed = jnp.transpose(cross[...])
        if sweep == 0:
            for c in range(3):
                n_k[c] = packed[8 * (FIELDS + c) : 8 * (FIELDS + c) + 8]
        edge = [packed[8 * v : 8 * v + 8] for v in range(FIELDS)]
        behind = [jnp.where(top_k, pltpu.roll(e, 1, 0), pltpu.roll(e, 7, 0)) for e in edge]
        half = jnp.where(top_k, 0.5, -0.5)
        send, keep, far = face_terms(edge, behind, [n_k[c] for c in range(3)], half)
        for v in range(FIELDS):
            next_rows = jnp.where(top_k, pltpu.roll(far[v], 7, 0), pltpu.roll(far[v], 1, 0))
            send_k[sweep, v] = rows(jnp.where(outer_k, send[v], next_rows), row_swap)
            keep_k[v] = jnp.where(outer_k, keep[v], next_rows)

    def interior():
        first_j, last_j = sub == 0, sub == NJ - 1
        first_k, last_k = lane == 0, lane == NK - 1

        def slab(i, carry):
            at = pl.multiple_of(i * NJ, NJ)
            g = [u[v, pl.ds(2 * NJ + at, NJ), :] for v in range(FIELDS)]
            nn = [n[c, pl.ds(at, NJ), :] for c in range(9)]
            inv, pressure = thermo(g)
            f = flux(g, inv, pressure, nn[0:3])
            for v in range(FIELDS):
                gi[v, pl.ds(NJ + at, NJ), :] = 0.5 * f[v]
            total = [-18.0 * damping * g[v] for v in range(FIELDS)]
            for d, axis, length, first, last in (
                (1, 0, NJ, first_j, last_j), (2, 1, NK, first_k, last_k),
            ):
                f = flux(g, inv, pressure, nn[3 * d : 3 * d + 3])
                for v in range(FIELDS):
                    def above(x):
                        return jnp.where(last, 0.0, pltpu.roll(x, length - 1, axis))

                    def below(x):
                        return jnp.where(first, 0.0, pltpu.roll(x, 1, axis))

                    smooth, half = 4.0 * damping * g[v], 0.5 * f[v]
                    up = smooth - half - damping * above(g[v])
                    down = smooth + half - damping * below(g[v])
                    total[v] = total[v] + above(up) + below(down)
            for v in range(FIELDS):
                r[v, pl.ds(at, NJ), :] = total[v]
            return carry

        lax.fori_loop(0, NI, slab, 0)

        def chord(i, carry):
            at = pl.multiple_of(i * NJ, NJ)
            for v in range(FIELDS):
                layer = [u[v, pl.ds(at + q * NJ, NJ), :] for q in (0, 1, 3, 4)]
                r[v, pl.ds(at, NJ), :] = (
                    r[v, pl.ds(at, NJ), :]
                    + gi[v, pl.ds(at, NJ), :]
                    - gi[v, pl.ds(at + 2 * NJ, NJ), :]
                    + 4.0 * damping * (layer[1] + layer[2])
                    - damping * (layer[0] + layer[3])
                )
            return carry

        lax.fori_loop(0, NI, chord, 0)

    def halo_k(sweep):
        for side in range(2):
            copies[sweep][2][1 - side].wait_recv()
        flip_i = jnp.bitwise_and(jnp.where(top_k, code[5], code[4]) - 1, 1) == 1
        flip_j = jnp.bitwise_and(jnp.where(top_k, code[5], code[4]) - 1, 2) == 2
        linked = jnp.where(top_k, code[5], code[4]) > 0
        for v in range(FIELDS):
            z = jnp.where(top_k, recv_k[sweep, 1, v], recv_k[sweep, 0, v])
            z = jnp.where(flip_i, lanes(z, lane_rev_i), z)
            z = jnp.where(flip_j, lanes(z, lane_rev_j), z)
            cross[pl.ds(8 * v, 8), :] = jnp.where(linked, z, keep_k[v])
        spread = jnp.transpose(cross[...])
        for i in range(NI):
            part = pl.ds(i * NJ, NJ)
            x = spread[i * NJ : (i + 1) * NJ]
            for v in range(FIELDS):
                r[v, part, :] = r[v, part, :] + jnp.where(
                    last_k4, pltpu.roll(x, NK - 2 - 8 * v, 1), 0.0
                )

    def halo_i(sweep):
        for side in range(2):
            copies[sweep][0][1 - side].wait_recv()
            face = side
            for q in range(2 * FIELDS):
                v = q % FIELDS
                x = recv_i[sweep, side, q]
                x = jnp.where(bit0[face], rows(x, row_rev), x)
                x = jnp.where(bit1[face], lanes(x, lane_rev), x)
                own = keep_i[side, v] if q < FIELDS else send_i[sweep, side, q]
                x = jnp.where(joined[face], x, own)
                depth = 0 if q < FIELDS else 1
                at = (depth if side == 0 else NI - 1 - depth) * NJ
                r[v, pl.ds(at, NJ), :] = r[v, pl.ds(at, NJ), :] + x

    def halo_j(sweep):
        for side in range(2):
            copies[sweep][1][1 - side].wait_recv()
            face = 2 + side
            for q in range(2 * FIELDS):
                v = q % FIELDS
                x = [recv_j[sweep, side, q, pl.ds(8 * h, 8), :] for h in range(2)]
                rev = [rows(x[1 - h], row_rev) for h in range(2)]
                x = [jnp.where(bit0[face], rev[h], x[h]) for h in range(2)]
                x = [jnp.where(bit1[face], lanes(x[h], lane_rev), x[h]) for h in range(2)]
                depth = 0 if q < FIELDS else 1
                at = depth if side == 0 else NJ - 1 - depth
                for h in range(2):
                    part = pl.ds(8 * h, 8)
                    own = keep_j[side, v, part, :] if q < FIELDS else send_j[sweep, side, q, part, :]
                    y = jnp.where(joined[face], x[h], own)
                    where = pl.ds(8 * h * NJ + at, 8, stride=NJ)
                    r[v, where, :] = r[v, where, :] + y

    def prepare():
        for load in load_rest[1:]:
            load.wait()
        high, low = halves(jnp.transpose(inv_k[...]))
        for h in range(2):
            w_k[pl.ds(h * NK, NK), pl.ds(0, NK)] = high
            w_k[pl.ds(h * NK, NK), pl.ds(NK, NK)] = low
        wide = lax.broadcasted_iota(jnp.int32, (CELLS, NI), 0)
        e_i = jnp.where(
            lax.shift_right_logical(wide, 3)
            == lax.broadcasted_iota(jnp.int32, (CELLS, NI), 1), 1.0, 0.0,
        ).astype(jnp.float32)
        wide = lax.broadcasted_iota(jnp.int32, (CELLS, NJ), 0)
        e_j = jnp.where(
            jnp.bitwise_and(wide, 7) == lax.broadcasted_iota(jnp.int32, (CELLS, NJ), 1), 1.0, 0.0
        ).astype(jnp.float32)
        big_i = dot(dot(e_i, inv_i[...], ((1,), (0,))), e_i, ((1,), (1,)))
        big_j = dot(dot(e_j, inv_j[...], ((1,), (0,))), e_j, ((1,), (1,)))
        high, low = halves(big_i * big_j)
        m2[:, pl.ds(0, CELLS)] = high
        m2[:, pl.ds(CELLS, CELLS)] = low

    def solve(sweep):
        for v in range(FIELDS):
            high, low = halves(r[v])
            r2[v, :, pl.ds(0, NK)] = high
            r2[v, :, pl.ds(NK, NK)] = low
        t = product(r2[...].reshape(FIELDS * CELLS, 2 * NK), w_k[...])
        for v in range(FIELDS):
            high, low = halves(t[v * CELLS : (v + 1) * CELLS])
            w = jnp.concatenate([high, low], axis=1)
            change = product(m2[...], jnp.concatenate([w, w], axis=0))
            if sweep == 0:
                out[v] = change
                inner = pl.ds(2 * NJ, CELLS)
                u[v, inner, :] = u[v, inner, :] + pseudo_step * change
            else:
                out[v] = out[v] + change

    for sweep in range(SWEEPS):
        edge_j(sweep)
        if sweep == 0:
            pl.semaphore_wait(barrier, 6)
        for side in range(2):
            copies[sweep][1][side].start()
        edge_i(sweep)
        for side in range(2):
            copies[sweep][0][side].start()
        edge_k(sweep)
        for side in range(2):
            copies[sweep][2][side].start()
        interior()
        if sweep == 0:
            prepare()
            load_rest[0].wait()
            code, bit0, bit1, joined = read_codes()
        halo_k(sweep)
        halo_i(sweep)
        halo_j(sweep)
        solve(sweep)

    for sweep in range(SWEEPS):
        for d in range(3):
            for side in range(2):
                copies[sweep][d][side].wait_send()


def local(state, metrics, face_codes, inverse_i, inverse_j, inverse_k):
    f32 = jnp.float32
    vmem = pl.BlockSpec(memory_space=pltpu.VMEM)
    hbm = pl.BlockSpec(memory_space=pltpu.HBM)
    result = pl.pallas_call(
        kernel,
        out_shape=jax.ShapeDtypeStruct((FIELDS, CELLS, NK), f32),
        in_specs=[hbm] * 6,
        out_specs=vmem,
        scratch_shapes=[
            pltpu.SMEM((1, 6), jnp.int32),
            pltpu.VMEM((FIELDS, CELLS + 4 * NJ, NK), f32),
            pltpu.VMEM((9, CELLS, NK), f32),
            pltpu.VMEM((NI, NI), f32),
            pltpu.VMEM((NJ, NJ), f32),
            pltpu.VMEM((NK, NK), f32),
            pltpu.VMEM((FIELDS, CELLS, NK), f32),
            pltpu.VMEM((FIELDS, CELLS + 2 * NJ, NK), f32),
            pltpu.VMEM((FIELDS, CELLS, 2 * NK), BF16),
            pltpu.VMEM((2 * NK, 2 * NK), BF16),
            pltpu.VMEM((CELLS, 2 * CELLS), BF16),
            pltpu.VMEM((CELLS, NK), f32),
            pltpu.VMEM((3, 8, NK), f32),
            pltpu.VMEM((SWEEPS, 2, 2 * FIELDS, NJ, NK), f32),
            pltpu.VMEM((SWEEPS, 2, 2 * FIELDS, NI, NK), f32),
            pltpu.VMEM((SWEEPS, FIELDS, 8, NK), f32),
            pltpu.VMEM((2, FIELDS, NJ, NK), f32),
            pltpu.VMEM((2, FIELDS, NI, NK), f32),
            pltpu.VMEM((FIELDS, 8, NK), f32),
            pltpu.VMEM((SWEEPS, 2, 2 * FIELDS, NJ, NK), f32),
            pltpu.VMEM((SWEEPS, 2, 2 * FIELDS, NI, NK), f32),
            pltpu.VMEM((SWEEPS, 2, FIELDS, 8, NK), f32),
            pltpu.SemaphoreType.DMA((6,)),
            pltpu.SemaphoreType.DMA((SWEEPS, 3, 2)),
            pltpu.SemaphoreType.DMA((SWEEPS, 3, 2)),
        ],
        compiler_params=pltpu.CompilerParams(
            collective_id=0, has_side_effects=True, vmem_limit_bytes=12 * 2**20
        ),
        name="adi",
    )(*(
        pltpu.with_memory_space_constraint(x, pltpu.HBM)
        for x in (
            face_codes.reshape(1, 6),
            state.reshape(FIELDS, CELLS, NK),
            metrics.reshape(9, CELLS, NK),
            inverse_i.reshape(NI, NI),
            inverse_j.reshape(NJ, NJ),
            inverse_k.reshape(NK, NK),
        )
    ))
    return result.reshape(state.shape)


def solution(mesh):
    cells = P(None, "chord", "normal", "span")
    block = P("chord", "normal", "span", None, None)
    return jax.shard_map(
        local,
        mesh=mesh,
        in_specs=(cells, cells, P("chord", "normal", "span", None), block, block, block),
        out_specs=cells,
        check_vma=False,
    )
```

```python
import functools

import jax
import jax.numpy as jnp
from jax import lax
from jax.experimental import pallas as pl
from jax.experimental.pallas import tpu as pltpu
from jax.sharding import PartitionSpec as P

MESH = pl.DeviceIdType.MESH
HIGHEST = lax.Precision.HIGHEST
BF16 = jnp.bfloat16
AXES = ("chord", "normal", "span")
SWEEPS = 2
FIELDS = 5
NI, NJ, NK = 16, 8, 128
CELLS = NI * NJ
LATE = 4 * NJ + 2 * NI

gas_factor = 0.4
damping = 0.1
pseudo_step = 0.03


def dot(a, b, contract):
    return lax.dot_general(
        a, b, (contract, ((), ())), precision=HIGHEST, preferred_element_type=jnp.float32
    )


def thermo(g):
    inv = 1.0 / g[0]
    kinetic = 0.5 * (g[1] * g[1] + g[2] * g[2] + g[3] * g[3]) * inv
    pressure = gas_factor * (g[4] - kinetic)
    return inv, pressure


def flux(g, inv, pressure, n):
    speed = (n[0] * g[1] + n[1] * g[2] + n[2] * g[3]) * inv
    return [
        g[0] * speed,
        g[1] * speed + n[0] * pressure,
        g[2] * speed + n[1] * pressure,
        g[3] * speed + n[2] * pressure,
        (g[4] + pressure) * speed,
    ]


def face_terms(edge, behind, n, half):
    inv, pressure = thermo(edge)
    f = flux(edge, inv, pressure, n)
    send, keep, far = [], [], []
    for v in range(FIELDS):
        smooth = 4.0 * damping * edge[v] - damping * behind[v]
        send.append(smooth + half * f[v])
        keep.append(smooth - half * f[v])
        far.append(-damping * edge[v])
    return send, keep, far


def halves(x):
    high = x.astype(BF16)
    return high, (x - high.astype(jnp.float32)).astype(BF16)


def product(a, b):
    return lax.dot_general(a, b, (((1,), (0,)), ((), ())), preferred_element_type=jnp.float32)


def lanes(x, index):
    return jnp.take_along_axis(x, index, axis=1, mode="promise_in_bounds")


def rows(x, index):
    return jnp.take_along_axis(x, index, axis=0, mode="promise_in_bounds")


def kernel(
    codes_hbm, state, metrics, inv_i_hbm, inv_j_hbm, inv_k_hbm, out,
    codes, u, n, inv_i, inv_j, inv_k, r, late, gi, w_k, m3, late3, cross, n_k,
    send_i, send_j, send_k, keep_i, keep_j, keep_k, recv_i, recv_j, recv_k,
    load_sem, send_sem, recv_sem,
):
    load_u = pltpu.make_async_copy(state, u.at[:, pl.ds(2 * NJ, CELLS), :], load_sem.at[0])
    load_n = pltpu.make_async_copy(metrics, n, load_sem.at[1])
    load_rest = [
        pltpu.make_async_copy(a, b, load_sem.at[2 + q])
        for q, (a, b) in enumerate((
            (codes_hbm, codes), (inv_i_hbm, inv_i), (inv_j_hbm, inv_j), (inv_k_hbm, inv_k),
        ))
    ]
    load_u.start()
    load_n.start()
    for load in load_rest:
        load.start()

    size = [lax.axis_size(axis) for axis in AXES]
    me = [lax.axis_index(axis) for axis in AXES]

    def neighbour(d, side):
        return lax.rem(me[d] + size[d] - 1 + 2 * side, size[d])

    barrier = pltpu.get_barrier_semaphore()
    for d, axis in enumerate(AXES):
        for side in range(2):
            pl.semaphore_signal(
                barrier, inc=1, device_id={axis: neighbour(d, side)}, device_id_type=MESH
            )

    sends = (send_i, send_j, send_k)
    recvs = (recv_i, recv_j, recv_k)
    far_side = [lax.rem(me[d], 2) for d in range(2)]

    def copy(sweep, d, side):
        return pltpu.make_async_remote_copy(
            src_ref=sends[d].at[sweep] if d == 2 else sends[d].at[sweep, side],
            dst_ref=recvs[d].at[sweep, 1 - side],
            send_sem=send_sem.at[sweep, d, side],
            recv_sem=recv_sem.at[sweep, d, 1 - side],
            device_id={AXES[d]: neighbour(d, side)},
            device_id_type=MESH,
        )

    sub = lax.broadcasted_iota(jnp.int32, (8, NK), 0)
    lane = lax.broadcasted_iota(jnp.int32, (8, NK), 1)
    lane_rev = NK - 1 - lane
    row_rev = 7 - sub
    row_swap = jnp.where(sub < 4, 3 - sub, sub)
    outer_k = jnp.logical_or(sub == 1, sub == 2)
    top_k = sub < 2
    last_k4 = jnp.logical_or(lane < 2, lane >= NK - 2)
    lane_rev_i = jnp.bitwise_xor(lane, CELLS - NJ)
    lane_rev_j = jnp.bitwise_xor(lane, NJ - 1)

    zero = jnp.zeros((2 * NJ, NK), jnp.float32)
    for v in range(FIELDS):
        u[v, pl.ds(0, 2 * NJ), :] = zero
        u[v, pl.ds(2 * NJ + CELLS, 2 * NJ), :] = zero
        gi[v, pl.ds(0, NJ), :] = zero[:NJ]
        gi[v, pl.ds(NJ + CELLS, NJ), :] = zero[:NJ]
    cross[...] = jnp.zeros((CELLS, NK), jnp.float32)

    load_u.wait()
    load_n.wait()

    def edge_i(sweep):
        for side in range(2):
            at = 0 if side == 0 else NI - 1
            back = 1 if side == 0 else NI - 2
            edge = [u[v, pl.ds((2 + at) * NJ, NJ), :] for v in range(FIELDS)]
            behind = [u[v, pl.ds((2 + back) * NJ, NJ), :] for v in range(FIELDS)]
            nn = [n[c, pl.ds(at * NJ, NJ), :] for c in range(3)]
            send, keep, far = face_terms(edge, behind, nn, -0.5 if side == 0 else 0.5)
            for v in range(FIELDS):
                send_i[sweep, side, v] = send[v]
                send_i[sweep, side, FIELDS + v] = far[v]
                keep_i[side, v] = keep[v]

    def edge_j(sweep):
        for side in range(2):
            at = 0 if side == 0 else NJ - 1
            back = 1 if side == 0 else NJ - 2
            edge = [u[v, pl.ds(2 * NJ + at, NI, stride=NJ), :] for v in range(FIELDS)]
            behind = [u[v, pl.ds(2 * NJ + back, NI, stride=NJ), :] for v in range(FIELDS)]
            nn = [n[3 + c, pl.ds(at, NI, stride=NJ), :] for c in range(3)]
            send, keep, far = face_terms(edge, behind, nn, -0.5 if side == 0 else 0.5)
            for v in range(FIELDS):
                send_j[sweep, side, v] = send[v]
                send_j[sweep, side, FIELDS + v] = far[v]
                keep_j[side, v] = keep[v]

    def edge_k(sweep):
        for i in range(NI):
            x = [u[v, pl.ds((2 + i) * NJ, NJ), :] for v in range(FIELDS)]
            if sweep == 0:
                x = x + [n[6 + c, pl.ds(i * NJ, NJ), :] for c in range(3)]
            y = pltpu.roll(x[0], 2, 1)
            for v in range(1, len(x)):
                y = jnp.where(lane >= 8 * v, pltpu.roll(x[v], 8 * v + 2, 1), y)
            cross[pl.ds(i * NJ, NJ), :] = y
        packed = jnp.transpose(cross[...])
        if sweep == 0:
            for c in range(3):
                n_k[c] = packed[8 * (FIELDS + c) : 8 * (FIELDS + c) + 8]
        edge = [packed[8 * v : 8 * v + 8] for v in range(FIELDS)]
        behind = [jnp.where(top_k, pltpu.roll(e, 1, 0), pltpu.roll(e, 7, 0)) for e in edge]
        half = jnp.where(top_k, 0.5, -0.5)
        send, keep, far = face_terms(edge, behind, [n_k[c] for c in range(3)], half)
        for v in range(FIELDS):
            next_rows = jnp.where(top_k, pltpu.roll(far[v], 7, 0), pltpu.roll(far[v], 1, 0))
            send_k[sweep, v] = rows(jnp.where(outer_k, send[v], next_rows), row_swap)
            keep_k[v] = jnp.where(outer_k, keep[v], next_rows)

    def interior():
        first_j, last_j = sub == 0, sub == NJ - 1
        first_k, last_k = lane == 0, lane == NK - 1

        def slab(i, carry):
            at = pl.multiple_of(i * NJ, NJ)
            g = [u[v, pl.ds(2 * NJ + at, NJ), :] for v in range(FIELDS)]
            nn = [n[c, pl.ds(at, NJ), :] for c in range(9)]
            inv, pressure = thermo(g)
            f = flux(g, inv, pressure, nn[0:3])
            for v in range(FIELDS):
                gi[v, pl.ds(NJ + at, NJ), :] = 0.5 * f[v]
            total = [-18.0 * damping * g[v] for v in range(FIELDS)]
            for d, axis, length, first, last in (
                (1, 0, NJ, first_j, last_j), (2, 1, NK, first_k, last_k),
            ):
                f = flux(g, inv, pressure, nn[3 * d : 3 * d + 3])
                for v in range(FIELDS):
                    def above(x):
                        return jnp.where(last, 0.0, pltpu.roll(x, length - 1, axis))

                    def below(x):
                        return jnp.where(first, 0.0, pltpu.roll(x, 1, axis))

                    smooth, half = 4.0 * damping * g[v], 0.5 * f[v]
                    up = smooth - half - damping * above(g[v])
                    down = smooth + half - damping * below(g[v])
                    total[v] = total[v] + above(up) + below(down)
            for v in range(FIELDS):
                r[v, pl.ds(at, NJ), :] = total[v]
            return carry

        lax.fori_loop(0, NI, slab, 0, unroll=4)

        def chord(i, carry):
            at = pl.multiple_of(i * NJ, NJ)
            for v in range(FIELDS):
                layer = [u[v, pl.ds(at + q * NJ, NJ), :] for q in (0, 1, 3, 4)]
                r[v, pl.ds(at, NJ), :] = (
                    r[v, pl.ds(at, NJ), :]
                    + gi[v, pl.ds(at, NJ), :]
                    - gi[v, pl.ds(at + 2 * NJ, NJ), :]
                    + 4.0 * damping * (layer[1] + layer[2])
                    - damping * (layer[0] + layer[3])
                )
            return carry

        lax.fori_loop(0, NI, chord, 0, unroll=4)

    def halo_k(sweep):
        for side in range(2):
            copy(sweep, 2, side).wait_recv()
        code = [jnp.full((8, NK), codes[0, q], jnp.int32) for q in range(4, 6)]
        flip_i = jnp.bitwise_and(jnp.where(top_k, code[1], code[0]) - 1, 1) == 1
        flip_j = jnp.bitwise_and(jnp.where(top_k, code[1], code[0]) - 1, 2) == 2
        linked = jnp.where(top_k, code[1], code[0]) > 0
        for v in range(FIELDS):
            z = jnp.where(top_k, recv_k[sweep, 1, v], recv_k[sweep, 0, v])
            z = jnp.where(flip_i, lanes(z, lane_rev_i), z)
            z = jnp.where(flip_j, lanes(z, lane_rev_j), z)
            cross[pl.ds(8 * v, 8), :] = jnp.where(linked, z, keep_k[v])
        spread = jnp.transpose(cross[...])
        for i in range(NI):
            part = pl.ds(i * NJ, NJ)
            x = spread[i * NJ : (i + 1) * NJ]
            for v in range(FIELDS):
                r[v, part, :] = r[v, part, :] + jnp.where(
                    last_k4, pltpu.roll(x, NK - 2 - 8 * v, 1), 0.0
                )

    def orientation(d, side):
        code = jnp.full((8, NK), codes[0, 2 * d + side], jnp.int32)
        first = jnp.bitwise_and(code - 1, 1) == 1
        second = jnp.bitwise_and(code - 1, 2) == 2
        return first, second, code > 0

    def halo_i(sweep, side):
        copy(sweep, 0, 1 - side).wait_recv()
        first, second, linked = orientation(0, side)
        for q in range(2 * FIELDS):
            v = q % FIELDS
            x = recv_i[sweep, side, q]
            x = jnp.where(first, rows(x, row_rev), x)
            x = jnp.where(second, lanes(x, lane_rev), x)
            own = keep_i[side, v] if q < FIELDS else send_i[sweep, side, q]
            x = jnp.where(linked, x, own)
            depth = 0 if q < FIELDS else 1
            at = pl.multiple_of((2 * side + depth) * NJ, NJ)
            late[v, pl.ds(at, NJ), :] = x

    def halo_j(sweep, side, far):
        copy(sweep, 1, 1 - side).wait_recv()
        first, second, linked = orientation(1, side)
        for q in range(2 * FIELDS):
            v = q % FIELDS
            x = [recv_j[sweep, side, q, pl.ds(8 * h, 8), :] for h in range(2)]
            rev = [rows(x[1 - h], row_rev) for h in range(2)]
            x = [jnp.where(first, rev[h], x[h]) for h in range(2)]
            x = [jnp.where(second, lanes(x[h], lane_rev), x[h]) for h in range(2)]
            depth = 0 if q < FIELDS else 1
            at = side * (NJ - 1) + (1 - 2 * side) * depth
            for h in range(2):
                part = pl.ds(8 * h, 8)
                own = keep_j[side, v, part, :] if q < FIELDS else send_j[sweep, side, q, part, :]
                y = jnp.where(linked, x[h], own)
                if far:
                    late[v, pl.ds(4 * NJ + depth * NI + 8 * h, 8), :] = y
                else:
                    where = pl.ds(8 * h * NJ + at, 8, stride=NJ)
                    r[v, where, :] = r[v, where, :] + y

    def prepare():
        for load in load_rest[1:]:
            load.wait()
        high, low = halves(jnp.transpose(inv_k[...]))
        for h, part in enumerate((high, high, low)):
            w_k[pl.ds(h * NK, NK), :] = part
        def one_hot(index, shape):
            return jnp.where(index == lax.broadcasted_iota(jnp.int32, shape, 1), 1.0, 0.0).astype(
                jnp.float32
            )

        def taken(one, x):
            high, low = halves(x)
            return product(
                jnp.concatenate([one, one], axis=1).astype(BF16), jnp.concatenate([high, low], axis=0)
            )

        def pair(block_i, block_j):
            return taken(all_i, jnp.transpose(taken(block_i, t_i))) * taken(
                all_j, jnp.transpose(taken(block_j, t_j))
            )

        cell = lax.broadcasted_iota(jnp.int32, (CELLS, NI), 0)
        all_i = one_hot(lax.shift_right_logical(cell, 3), (CELLS, NI))
        cell = lax.broadcasted_iota(jnp.int32, (CELLS, NJ), 0)
        all_j = one_hot(jnp.bitwise_and(cell, 7), (CELLS, NJ))
        t_i = jnp.transpose(inv_i[...])
        t_j = jnp.transpose(inv_j[...])
        q = lax.broadcasted_iota(jnp.int32, (LATE, NI), 0)
        layer = lax.shift_right_logical(q, 3)
        edge = jnp.where(layer < 2, layer, NI + 1 - layer)
        late_i = one_hot(jnp.where(q < 4 * NJ, edge, jnp.bitwise_and(q, NI - 1)), (LATE, NI))
        q = lax.broadcasted_iota(jnp.int32, (LATE, NJ), 0)
        depth = jnp.where(q < 4 * NJ + NI, 0, 1)
        edge = far_side[1] * (NJ - 1) + (1 - 2 * far_side[1]) * depth
        late_j = one_hot(jnp.where(q < 4 * NJ, jnp.bitwise_and(q, 7), edge), (LATE, NJ))
        high, low = halves(pair(all_i, all_j))
        for h, part in enumerate((high, low, high)):
            m3[:, pl.ds(h * CELLS, CELLS)] = part
        high, low = halves(pair(late_i, late_j))
        late3[...] = jnp.concatenate([high, low, high], axis=1)

    def add(sweep, v, change, first):
        if sweep == 0 and first:
            out[v] = change
        else:
            out[v] = out[v] + change
        if sweep == 0:
            inner = pl.ds(2 * NJ, CELLS)
            u[v, inner, :] = u[v, inner, :] + pseudo_step * change

    def solve_late(sweep):
        high, low = halves(late[...].reshape(FIELDS * LATE, NK))
        t = product(jnp.concatenate([high, low, high], axis=1), w_k[...])
        for group in ((0, 1, 2, 3), (4,)):
            high, low = halves(
                jnp.concatenate([t[v * LATE : (v + 1) * LATE] for v in group], axis=1)
            )
            both = product(late3[...], jnp.concatenate([high, high, low], axis=0))
            for q, v in enumerate(group):
                add(sweep, v, both[:, q * NK : (q + 1) * NK], False)

    def solve(sweep):
        for group in ((0, 1), (2, 3), (4,)):
            high, low = halves(jnp.concatenate([r[v] for v in group], axis=0))
            t = product(jnp.concatenate([high, low, high], axis=1), w_k[...])
            high, low = halves(
                jnp.concatenate([t[q * CELLS : (q + 1) * CELLS] for q in range(len(group))], axis=1)
            )
            both = product(m3[...], jnp.concatenate([high, high, low], axis=0))
            for q, v in enumerate(group):
                add(sweep, v, both[:, q * NK : (q + 1) * NK], True)

    for sweep in range(SWEEPS):
        edge_i(sweep)
        if sweep == 0:
            pl.semaphore_wait(barrier, 6)
        edge_j(sweep)
        copy(sweep, 1, far_side[1]).start()
        copy(sweep, 0, far_side[0]).start()
        edge_k(sweep)
        for side in range(2):
            copy(sweep, 2, side).start()
        copy(sweep, 0, 1 - far_side[0]).start()
        copy(sweep, 1, 1 - far_side[1]).start()
        interior()
        if sweep == 0:
            prepare()
            load_rest[0].wait()
        halo_j(sweep, 1 - far_side[1], False)
        halo_k(sweep)
        solve(sweep)
        halo_i(sweep, 1 - far_side[0])
        halo_j(sweep, far_side[1], True)
        halo_i(sweep, far_side[0])
        solve_late(sweep)

    for sweep in range(SWEEPS):
        for d in range(3):
            for side in range(2):
                copy(sweep, d, side).wait_send()


def local(state, metrics, face_codes, inverse_i, inverse_j, inverse_k):
    f32 = jnp.float32
    vmem = pl.BlockSpec(memory_space=pltpu.VMEM)
    hbm = pl.BlockSpec(memory_space=pltpu.HBM)
    result = pl.pallas_call(
        kernel,
        out_shape=jax.ShapeDtypeStruct((FIELDS, CELLS, NK), f32),
        in_specs=[hbm] * 6,
        out_specs=vmem,
        scratch_shapes=[
            pltpu.SMEM((1, 6), jnp.int32),
            pltpu.VMEM((FIELDS, CELLS + 4 * NJ, NK), f32),
            pltpu.VMEM((9, CELLS, NK), f32),
            pltpu.VMEM((NI, NI), f32),
            pltpu.VMEM((NJ, NJ), f32),
            pltpu.VMEM((NK, NK), f32),
            pltpu.VMEM((FIELDS, CELLS, NK), f32),
            pltpu.VMEM((FIELDS, LATE, NK), f32),
            pltpu.VMEM((FIELDS, CELLS + 2 * NJ, NK), f32),
            pltpu.VMEM((3 * NK, NK), BF16),
            pltpu.VMEM((CELLS, 3 * CELLS), BF16),
            pltpu.VMEM((CELLS, 3 * LATE), BF16),
            pltpu.VMEM((CELLS, NK), f32),
            pltpu.VMEM((3, 8, NK), f32),
            pltpu.VMEM((SWEEPS, 2, 2 * FIELDS, NJ, NK), f32),
            pltpu.VMEM((SWEEPS, 2, 2 * FIELDS, NI, NK), f32),
            pltpu.VMEM((SWEEPS, FIELDS, 8, NK), f32),
            pltpu.VMEM((2, FIELDS, NJ, NK), f32),
            pltpu.VMEM((2, FIELDS, NI, NK), f32),
            pltpu.VMEM((FIELDS, 8, NK), f32),
            pltpu.VMEM((SWEEPS, 2, 2 * FIELDS, NJ, NK), f32),
            pltpu.VMEM((SWEEPS, 2, 2 * FIELDS, NI, NK), f32),
            pltpu.VMEM((SWEEPS, 2, FIELDS, 8, NK), f32),
            pltpu.SemaphoreType.DMA((6,)),
            pltpu.SemaphoreType.DMA((SWEEPS, 3, 2)),
            pltpu.SemaphoreType.DMA((SWEEPS, 3, 2)),
        ],
        compiler_params=pltpu.CompilerParams(
            collective_id=0, has_side_effects=True, vmem_limit_bytes=12 * 2**20
        ),
        name="adi",
    )(*(
        pltpu.with_memory_space_constraint(x, pltpu.HBM)
        for x in (
            face_codes.reshape(1, 6),
            state.reshape(FIELDS, CELLS, NK),
            metrics.reshape(9, CELLS, NK),
            inverse_i.reshape(NI, NI),
            inverse_j.reshape(NJ, NJ),
            inverse_k.reshape(NK, NK),
        )
    ))
    return result.reshape(state.shape)


def solution(mesh):
    cells = P(None, "chord", "normal", "span")
    block = P("chord", "normal", "span", None, None)
    return jax.shard_map(
        local,
        mesh=mesh,
        in_specs=(cells, cells, P("chord", "normal", "span", None), block, block, block),
        out_specs=cells,
        check_vma=False,
    )
```

```python
import functools

import jax
import jax.numpy as jnp
from jax import lax
from jax.experimental import pallas as pl
from jax.experimental.pallas import tpu as pltpu
from jax.sharding import PartitionSpec as P

MESH = pl.DeviceIdType.MESH
HIGHEST = lax.Precision.HIGHEST
BF16 = jnp.bfloat16
AXES = ("chord", "normal", "span")
SWEEPS = 2
FIELDS = 5
NI, NJ, NK = 16, 8, 128
CELLS = NI * NJ
LATE = 4 * NJ + 2 * NI

gas_factor = 0.4
damping = 0.1
pseudo_step = 0.03


def dot(a, b, contract):
    return lax.dot_general(
        a, b, (contract, ((), ())), precision=HIGHEST, preferred_element_type=jnp.float32
    )


def thermo(g):
    inv = 1.0 / g[0]
    kinetic = 0.5 * (g[1] * g[1] + g[2] * g[2] + g[3] * g[3]) * inv
    pressure = gas_factor * (g[4] - kinetic)
    return inv, pressure


def flux(g, inv, pressure, n):
    speed = (n[0] * g[1] + n[1] * g[2] + n[2] * g[3]) * inv
    return [
        g[0] * speed,
        g[1] * speed + n[0] * pressure,
        g[2] * speed + n[1] * pressure,
        g[3] * speed + n[2] * pressure,
        (g[4] + pressure) * speed,
    ]


def face_terms(edge, behind, n, half):
    inv, pressure = thermo(edge)
    f = flux(edge, inv, pressure, n)
    send, keep, far = [], [], []
    for v in range(FIELDS):
        smooth = 4.0 * damping * edge[v] - damping * behind[v]
        send.append(smooth + half * f[v])
        keep.append(smooth - half * f[v])
        far.append(-damping * edge[v])
    return send, keep, far


def halves(x):
    high = x.astype(BF16)
    return high, (x - high.astype(jnp.float32)).astype(BF16)


def product(a, b):
    return lax.dot_general(a, b, (((1,), (0,)), ((), ())), preferred_element_type=jnp.float32)


def lanes(x, index):
    return jnp.take_along_axis(x, index, axis=1, mode="promise_in_bounds")


def rows(x, index):
    return jnp.take_along_axis(x, index, axis=0, mode="promise_in_bounds")


def kernel(
    codes_hbm, state, metrics, inv_i_hbm, inv_j_hbm, inv_k_hbm, out,
    codes, u, n, inv_i, inv_j, inv_k, r, late, gi, w_k, m3, late3, cross, n_k,
    send_i, send_j, send_k, keep_i, keep_j, keep_k, recv_i, recv_j, recv_k,
    load_sem, send_sem, recv_sem,
):
    load_u = pltpu.make_async_copy(state, u.at[:, pl.ds(2 * NJ, CELLS), :], load_sem.at[0])
    load_n = pltpu.make_async_copy(metrics, n, load_sem.at[1])
    load_rest = [
        pltpu.make_async_copy(a, b, load_sem.at[2 + q])
        for q, (a, b) in enumerate((
            (codes_hbm, codes), (inv_i_hbm, inv_i), (inv_j_hbm, inv_j), (inv_k_hbm, inv_k),
        ))
    ]
    for load in load_rest[::-1]:
        load.start()
    load_u.start()
    load_n.start()

    size = [lax.axis_size(axis) for axis in AXES]
    me = [lax.axis_index(axis) for axis in AXES]

    def neighbour(d, side):
        return lax.rem(me[d] + size[d] - 1 + 2 * side, size[d])

    barrier = pltpu.get_barrier_semaphore()
    for d, axis in enumerate(AXES):
        for side in range(2):
            pl.semaphore_signal(
                barrier, inc=1, device_id={axis: neighbour(d, side)}, device_id_type=MESH
            )

    sends = (send_i, send_j, send_k)
    recvs = (recv_i, recv_j, recv_k)
    far_side = [lax.rem(me[d], 2) for d in range(2)]

    def copy(sweep, d, side):
        return pltpu.make_async_remote_copy(
            src_ref=sends[d].at[sweep] if d == 2 else sends[d].at[sweep, side],
            dst_ref=recvs[d].at[sweep, 1 - side],
            send_sem=send_sem.at[sweep, d, side],
            recv_sem=recv_sem.at[sweep, d, 1 - side],
            device_id={AXES[d]: neighbour(d, side)},
            device_id_type=MESH,
        )

    sub = lax.broadcasted_iota(jnp.int32, (8, NK), 0)
    lane = lax.broadcasted_iota(jnp.int32, (8, NK), 1)
    lane_rev = NK - 1 - lane
    row_rev = 7 - sub
    row_swap = jnp.where(sub < 4, 3 - sub, sub)
    outer_k = jnp.logical_or(sub == 1, sub == 2)
    top_k = sub < 2
    last_k4 = jnp.logical_or(lane < 2, lane >= NK - 2)
    lane_rev_i = jnp.bitwise_xor(lane, CELLS - NJ)
    lane_rev_j = jnp.bitwise_xor(lane, NJ - 1)

    zero = jnp.zeros((2 * NJ, NK), jnp.float32)
    for v in range(FIELDS):
        u[v, pl.ds(0, 2 * NJ), :] = zero
        u[v, pl.ds(2 * NJ + CELLS, 2 * NJ), :] = zero
        gi[v, pl.ds(0, NJ), :] = zero[:NJ]
        gi[v, pl.ds(NJ + CELLS, NJ), :] = zero[:NJ]
    cross[...] = jnp.zeros((CELLS, NK), jnp.float32)

    def prepare():
        for load in load_rest[1:]:
            load.wait()
        high, low = halves(jnp.transpose(inv_k[...]))
        for h, part in enumerate((high, high, low)):
            w_k[pl.ds(h * NK, NK), :] = part
        def one_hot(index, shape):
            return jnp.where(index == lax.broadcasted_iota(jnp.int32, shape, 1), 1.0, 0.0).astype(
                jnp.float32
            )

        def taken(one, x):
            high, low = halves(x)
            return product(
                jnp.concatenate([one, one], axis=1).astype(BF16), jnp.concatenate([high, low], axis=0)
            )

        def pair(block_i, block_j):
            return taken(all_i, jnp.transpose(taken(block_i, t_i))) * taken(
                all_j, jnp.transpose(taken(block_j, t_j))
            )

        cell = lax.broadcasted_iota(jnp.int32, (CELLS, NI), 0)
        all_i = one_hot(lax.shift_right_logical(cell, 3), (CELLS, NI))
        cell = lax.broadcasted_iota(jnp.int32, (CELLS, NJ), 0)
        all_j = one_hot(jnp.bitwise_and(cell, 7), (CELLS, NJ))
        t_i = jnp.transpose(inv_i[...])
        t_j = jnp.transpose(inv_j[...])
        q = lax.broadcasted_iota(jnp.int32, (LATE, NI), 0)
        layer = lax.shift_right_logical(q, 3)
        edge = jnp.where(layer < 2, layer, NI + 1 - layer)
        late_i = one_hot(jnp.where(q < 4 * NJ, edge, jnp.bitwise_and(q, NI - 1)), (LATE, NI))
        q = lax.broadcasted_iota(jnp.int32, (LATE, NJ), 0)
        depth = jnp.where(q < 4 * NJ + NI, 0, 1)
        edge = far_side[1] * (NJ - 1) + (1 - 2 * far_side[1]) * depth
        late_j = one_hot(jnp.where(q < 4 * NJ, jnp.bitwise_and(q, 7), edge), (LATE, NJ))
        high, low = halves(pair(all_i, all_j))
        for h, part in enumerate((high, low, high)):
            m3[:, pl.ds(h * CELLS, CELLS)] = part
        high, low = halves(pair(late_i, late_j))
        late3[...] = jnp.concatenate([high, low, high], axis=1)

    prepare()
    load_rest[0].wait()
    load_u.wait()
    load_n.wait()

    def edge_i(sweep):
        for side in range(2):
            at = 0 if side == 0 else NI - 1
            back = 1 if side == 0 else NI - 2
            edge = [u[v, pl.ds((2 + at) * NJ, NJ), :] for v in range(FIELDS)]
            behind = [u[v, pl.ds((2 + back) * NJ, NJ), :] for v in range(FIELDS)]
            nn = [n[c, pl.ds(at * NJ, NJ), :] for c in range(3)]
            send, keep, far = face_terms(edge, behind, nn, -0.5 if side == 0 else 0.5)
            for v in range(FIELDS):
                send_i[sweep, side, v] = send[v]
                send_i[sweep, side, FIELDS + v] = far[v]
                keep_i[side, v] = keep[v]

    def edge_j(sweep):
        for side in range(2):
            at = 0 if side == 0 else NJ - 1
            back = 1 if side == 0 else NJ - 2
            edge = [u[v, pl.ds(2 * NJ + at, NI, stride=NJ), :] for v in range(FIELDS)]
            behind = [u[v, pl.ds(2 * NJ + back, NI, stride=NJ), :] for v in range(FIELDS)]
            nn = [n[3 + c, pl.ds(at, NI, stride=NJ), :] for c in range(3)]
            send, keep, far = face_terms(edge, behind, nn, -0.5 if side == 0 else 0.5)
            for v in range(FIELDS):
                send_j[sweep, side, v] = send[v]
                send_j[sweep, side, FIELDS + v] = far[v]
                keep_j[side, v] = keep[v]

    def edge_k(sweep):
        for i in range(NI):
            x = [u[v, pl.ds((2 + i) * NJ, NJ), :] for v in range(FIELDS)]
            if sweep == 0:
                x = x + [n[6 + c, pl.ds(i * NJ, NJ), :] for c in range(3)]
            y = pltpu.roll(x[0], 2, 1)
            for v in range(1, len(x)):
                y = jnp.where(lane >= 8 * v, pltpu.roll(x[v], 8 * v + 2, 1), y)
            cross[pl.ds(i * NJ, NJ), :] = y
        packed = jnp.transpose(cross[...])
        if sweep == 0:
            for c in range(3):
                n_k[c] = packed[8 * (FIELDS + c) : 8 * (FIELDS + c) + 8]
        edge = [packed[8 * v : 8 * v + 8] for v in range(FIELDS)]
        behind = [jnp.where(top_k, pltpu.roll(e, 1, 0), pltpu.roll(e, 7, 0)) for e in edge]
        half = jnp.where(top_k, 0.5, -0.5)
        send, keep, far = face_terms(edge, behind, [n_k[c] for c in range(3)], half)
        for v in range(FIELDS):
            next_rows = jnp.where(top_k, pltpu.roll(far[v], 7, 0), pltpu.roll(far[v], 1, 0))
            send_k[sweep, v] = rows(jnp.where(outer_k, send[v], next_rows), row_swap)
            keep_k[v] = jnp.where(outer_k, keep[v], next_rows)

    def interior():
        first_j, last_j = sub == 0, sub == NJ - 1
        first_k, last_k = lane == 0, lane == NK - 1

        def slab(i, carry):
            at = pl.multiple_of(i * NJ, NJ)
            g = [u[v, pl.ds(2 * NJ + at, NJ), :] for v in range(FIELDS)]
            nn = [n[c, pl.ds(at, NJ), :] for c in range(9)]
            inv, pressure = thermo(g)
            f = flux(g, inv, pressure, nn[0:3])
            for v in range(FIELDS):
                gi[v, pl.ds(NJ + at, NJ), :] = 0.5 * f[v]
            total = [-18.0 * damping * g[v] for v in range(FIELDS)]
            for d, axis, length, first, last in (
                (1, 0, NJ, first_j, last_j), (2, 1, NK, first_k, last_k),
            ):
                f = flux(g, inv, pressure, nn[3 * d : 3 * d + 3])
                for v in range(FIELDS):
                    def above(x):
                        return jnp.where(last, 0.0, pltpu.roll(x, length - 1, axis))

                    def below(x):
                        return jnp.where(first, 0.0, pltpu.roll(x, 1, axis))

                    smooth, half = 4.0 * damping * g[v], 0.5 * f[v]
                    up = smooth - half - damping * above(g[v])
                    down = smooth + half - damping * below(g[v])
                    total[v] = total[v] + above(up) + below(down)
            for v in range(FIELDS):
                r[v, pl.ds(at, NJ), :] = total[v]
            return carry

        lax.fori_loop(0, NI, slab, 0, unroll=4)

        def chord(i, carry):
            at = pl.multiple_of(i * NJ, NJ)
            for v in range(FIELDS):
                layer = [u[v, pl.ds(at + q * NJ, NJ), :] for q in (0, 1, 3, 4)]
                r[v, pl.ds(at, NJ), :] = (
                    r[v, pl.ds(at, NJ), :]
                    + gi[v, pl.ds(at, NJ), :]
                    - gi[v, pl.ds(at + 2 * NJ, NJ), :]
                    + 4.0 * damping * (layer[1] + layer[2])
                    - damping * (layer[0] + layer[3])
                )
            return carry

        lax.fori_loop(0, NI, chord, 0, unroll=4)

    def halo_k(sweep):
        for side in range(2):
            copy(sweep, 2, side).wait_recv()
        code = [jnp.full((8, NK), codes[0, q], jnp.int32) for q in range(4, 6)]
        flip_i = jnp.bitwise_and(jnp.where(top_k, code[1], code[0]) - 1, 1) == 1
        flip_j = jnp.bitwise_and(jnp.where(top_k, code[1], code[0]) - 1, 2) == 2
        linked = jnp.where(top_k, code[1], code[0]) > 0
        for v in range(FIELDS):
            z = jnp.where(top_k, recv_k[sweep, 1, v], recv_k[sweep, 0, v])
            z = jnp.where(flip_i, lanes(z, lane_rev_i), z)
            z = jnp.where(flip_j, lanes(z, lane_rev_j), z)
            cross[pl.ds(8 * v, 8), :] = jnp.where(linked, z, keep_k[v])
        spread = jnp.transpose(cross[...])
        for i in range(NI):
            part = pl.ds(i * NJ, NJ)
            x = spread[i * NJ : (i + 1) * NJ]
            for v in range(FIELDS):
                r[v, part, :] = r[v, part, :] + jnp.where(
                    last_k4, pltpu.roll(x, NK - 2 - 8 * v, 1), 0.0
                )

    def orientation(d, side):
        code = jnp.full((8, NK), codes[0, 2 * d + side], jnp.int32)
        first = jnp.bitwise_and(code - 1, 1) == 1
        second = jnp.bitwise_and(code - 1, 2) == 2
        return first, second, code > 0

    def halo_i(sweep, side):
        first, second, linked = orientation(0, side)
        for q in range(2 * FIELDS):
            v = q % FIELDS
            x = recv_i[sweep, side, q]
            x = jnp.where(first, rows(x, row_rev), x)
            x = jnp.where(second, lanes(x, lane_rev), x)
            own = keep_i[side, v] if q < FIELDS else send_i[sweep, side, q]
            x = jnp.where(linked, x, own)
            depth = 0 if q < FIELDS else 1
            at = pl.multiple_of((2 * side + depth) * NJ, NJ)
            late[v, pl.ds(at, NJ), :] = x

    def halo_j(sweep, side, far):
        if not far:
            copy(sweep, 1, 1 - side).wait_recv()
        first, second, linked = orientation(1, side)
        for q in range(2 * FIELDS):
            v = q % FIELDS
            x = [recv_j[sweep, side, q, pl.ds(8 * h, 8), :] for h in range(2)]
            rev = [rows(x[1 - h], row_rev) for h in range(2)]
            x = [jnp.where(first, rev[h], x[h]) for h in range(2)]
            x = [jnp.where(second, lanes(x[h], lane_rev), x[h]) for h in range(2)]
            depth = 0 if q < FIELDS else 1
            at = side * (NJ - 1) + (1 - 2 * side) * depth
            for h in range(2):
                part = pl.ds(8 * h, 8)
                own = keep_j[side, v, part, :] if q < FIELDS else send_j[sweep, side, q, part, :]
                y = jnp.where(linked, x[h], own)
                if far:
                    late[v, pl.ds(4 * NJ + depth * NI + 8 * h, 8), :] = y
                else:
                    where = pl.ds(8 * h * NJ + at, 8, stride=NJ)
                    r[v, where, :] = r[v, where, :] + y

    def add(sweep, v, change, first):
        if sweep == 0 and first:
            out[v] = change
        else:
            out[v] = out[v] + change
        if sweep == 0:
            inner = pl.ds(2 * NJ, CELLS)
            u[v, inner, :] = u[v, inner, :] + pseudo_step * change

    def solve_late(sweep):
        high, low = halves(late[...].reshape(FIELDS * LATE, NK))
        t = product(jnp.concatenate([high, low, high], axis=1), w_k[...])
        for group in ((0, 1, 2, 3), (4,)):
            high, low = halves(
                jnp.concatenate([t[v * LATE : (v + 1) * LATE] for v in group], axis=1)
            )
            both = product(late3[...], jnp.concatenate([high, high, low], axis=0))
            for q, v in enumerate(group):
                add(sweep, v, both[:, q * NK : (q + 1) * NK], False)

    def solve(sweep):
        for group in ((0, 1), (2, 3), (4,)):
            high, low = halves(jnp.concatenate([r[v] for v in group], axis=0))
            t = product(jnp.concatenate([high, low, high], axis=1), w_k[...])
            high, low = halves(
                jnp.concatenate([t[q * CELLS : (q + 1) * CELLS] for q in range(len(group))], axis=1)
            )
            both = product(m3[...], jnp.concatenate([high, high, low], axis=0))
            for q, v in enumerate(group):
                add(sweep, v, both[:, q * NK : (q + 1) * NK], True)

    for sweep in range(SWEEPS):
        edge_i(sweep)
        if sweep == 0:
            pl.semaphore_wait(barrier, 6)
        edge_j(sweep)
        copy(sweep, 1, far_side[1]).start()
        copy(sweep, 0, far_side[0]).start()
        edge_k(sweep)
        for side in range(2):
            copy(sweep, 2, side).start()
        copy(sweep, 0, 1 - far_side[0]).start()
        copy(sweep, 1, 1 - far_side[1]).start()
        interior()
        halo_j(sweep, 1 - far_side[1], False)
        halo_k(sweep)
        solve(sweep)
        copy(sweep, 0, 0).wait_recv()
        copy(sweep, 0, 1).wait_recv()
        copy(sweep, 1, 1 - far_side[1]).wait_recv()
        halo_i(sweep, 1 - far_side[0])
        halo_j(sweep, far_side[1], True)
        halo_i(sweep, far_side[0])
        solve_late(sweep)

    for sweep in range(SWEEPS):
        for d in range(3):
            for side in range(2):
                copy(sweep, d, side).wait_send()


def local(state, metrics, face_codes, inverse_i, inverse_j, inverse_k):
    f32 = jnp.float32
    vmem = pl.BlockSpec(memory_space=pltpu.VMEM)
    hbm = pl.BlockSpec(memory_space=pltpu.HBM)
    result = pl.pallas_call(
        kernel,
        out_shape=jax.ShapeDtypeStruct((FIELDS, CELLS, NK), f32),
        in_specs=[hbm] * 6,
        out_specs=vmem,
        scratch_shapes=[
            pltpu.SMEM((1, 6), jnp.int32),
            pltpu.VMEM((FIELDS, CELLS + 4 * NJ, NK), f32),
            pltpu.VMEM((9, CELLS, NK), f32),
            pltpu.VMEM((NI, NI), f32),
            pltpu.VMEM((NJ, NJ), f32),
            pltpu.VMEM((NK, NK), f32),
            pltpu.VMEM((FIELDS, CELLS, NK), f32),
            pltpu.VMEM((FIELDS, LATE, NK), f32),
            pltpu.VMEM((FIELDS, CELLS + 2 * NJ, NK), f32),
            pltpu.VMEM((3 * NK, NK), BF16),
            pltpu.VMEM((CELLS, 3 * CELLS), BF16),
            pltpu.VMEM((CELLS, 3 * LATE), BF16),
            pltpu.VMEM((CELLS, NK), f32),
            pltpu.VMEM((3, 8, NK), f32),
            pltpu.VMEM((SWEEPS, 2, 2 * FIELDS, NJ, NK), f32),
            pltpu.VMEM((SWEEPS, 2, 2 * FIELDS, NI, NK), f32),
            pltpu.VMEM((SWEEPS, FIELDS, 8, NK), f32),
            pltpu.VMEM((2, FIELDS, NJ, NK), f32),
            pltpu.VMEM((2, FIELDS, NI, NK), f32),
            pltpu.VMEM((FIELDS, 8, NK), f32),
            pltpu.VMEM((SWEEPS, 2, 2 * FIELDS, NJ, NK), f32),
            pltpu.VMEM((SWEEPS, 2, 2 * FIELDS, NI, NK), f32),
            pltpu.VMEM((SWEEPS, 2, FIELDS, 8, NK), f32),
            pltpu.SemaphoreType.DMA((6,)),
            pltpu.SemaphoreType.DMA((SWEEPS, 3, 2)),
            pltpu.SemaphoreType.DMA((SWEEPS, 3, 2)),
        ],
        compiler_params=pltpu.CompilerParams(
            collective_id=0, has_side_effects=True, vmem_limit_bytes=12 * 2**20
        ),
        name="adi",
    )(*(
        pltpu.with_memory_space_constraint(x, pltpu.HBM)
        for x in (
            face_codes.reshape(1, 6),
            state.reshape(FIELDS, CELLS, NK),
            metrics.reshape(9, CELLS, NK),
            inverse_i.reshape(NI, NI),
            inverse_j.reshape(NJ, NJ),
            inverse_k.reshape(NK, NK),
        )
    ))
    return result.reshape(state.shape)


def solution(mesh):
    cells = P(None, "chord", "normal", "span")
    block = P("chord", "normal", "span", None, None)
    return jax.shard_map(
        local,
        mesh=mesh,
        in_specs=(cells, cells, P("chord", "normal", "span", None), block, block, block),
        out_specs=cells,
        check_vma=False,
    )
```

```python
import functools

import jax
import jax.numpy as jnp
from jax import lax
from jax.experimental import pallas as pl
from jax.experimental.pallas import tpu as pltpu
from jax.sharding import PartitionSpec as P

MESH = pl.DeviceIdType.MESH
HIGHEST = lax.Precision.HIGHEST
BF16 = jnp.bfloat16
AXES = ("chord", "normal", "span")
SWEEPS = 2
FIELDS = 5
NI, NJ, NK = 16, 8, 128
CELLS = NI * NJ
LATE = 4 * NJ + 2 * NI

gas_factor = 0.4
damping = 0.1
pseudo_step = 0.03


def dot(a, b, contract):
    return lax.dot_general(
        a, b, (contract, ((), ())), precision=HIGHEST, preferred_element_type=jnp.float32
    )


def thermo(g):
    inv = 1.0 / g[0]
    kinetic = 0.5 * (g[1] * g[1] + g[2] * g[2] + g[3] * g[3]) * inv
    pressure = gas_factor * (g[4] - kinetic)
    return inv, pressure


def flux(g, inv, pressure, n):
    speed = (n[0] * g[1] + n[1] * g[2] + n[2] * g[3]) * inv
    return [
        g[0] * speed,
        g[1] * speed + n[0] * pressure,
        g[2] * speed + n[1] * pressure,
        g[3] * speed + n[2] * pressure,
        (g[4] + pressure) * speed,
    ]


def face_terms(edge, behind, n, half):
    inv, pressure = thermo(edge)
    f = flux(edge, inv, pressure, n)
    send, keep, far = [], [], []
    for v in range(FIELDS):
        smooth = 4.0 * damping * edge[v] - damping * behind[v]
        send.append(smooth + half * f[v])
        keep.append(smooth - half * f[v])
        far.append(-damping * edge[v])
    return send, keep, far


def halves(x):
    high = x.astype(BF16)
    return high, (x - high.astype(jnp.float32)).astype(BF16)


def product(a, b):
    return lax.dot_general(a, b, (((1,), (0,)), ((), ())), preferred_element_type=jnp.float32)


def lanes(x, index):
    return jnp.take_along_axis(x, index, axis=1, mode="promise_in_bounds")


def rows(x, index):
    return jnp.take_along_axis(x, index, axis=0, mode="promise_in_bounds")


def kernel(
    codes_hbm, state, metrics, inv_i_hbm, inv_j_hbm, inv_k_hbm, out,
    codes, u, n, inv_i, inv_j, inv_k, r, late, gi, w_k, m3, late3, cross, n_k,
    send_i, send_j, send_k, keep_i, keep_j, keep_k, recv_i, recv_j, recv_k,
    load_sem, send_sem, recv_sem,
):
    load_u = pltpu.make_async_copy(state, u.at[:, pl.ds(2 * NJ, CELLS), :], load_sem.at[0])
    load_n = pltpu.make_async_copy(metrics, n, load_sem.at[1])
    load_rest = [
        pltpu.make_async_copy(a, b, load_sem.at[2 + q])
        for q, (a, b) in enumerate((
            (codes_hbm, codes), (inv_i_hbm, inv_i), (inv_j_hbm, inv_j), (inv_k_hbm, inv_k),
        ))
    ]

    size = [lax.axis_size(axis) for axis in AXES]
    me = [lax.axis_index(axis) for axis in AXES]

    def neighbour(d, side):
        return lax.rem(me[d] + size[d] - 1 + 2 * side, size[d])

    barrier = pltpu.get_barrier_semaphore()
    for d, axis in enumerate(AXES):
        for side in range(2):
            pl.semaphore_signal(
                barrier, inc=1, device_id={axis: neighbour(d, side)}, device_id_type=MESH
            )

    for load in load_rest[::-1]:
        load.start()
    load_u.start()
    load_n.start()
    sends = (send_i, send_j, send_k)
    recvs = (recv_i, recv_j, recv_k)
    far_side = [lax.rem(me[d], 2) for d in range(2)]

    def copy(sweep, d, side):
        return pltpu.make_async_remote_copy(
            src_ref=sends[d].at[sweep] if d == 2 else sends[d].at[sweep, side],
            dst_ref=recvs[d].at[sweep, 1 - side],
            send_sem=send_sem.at[sweep, d, side],
            recv_sem=recv_sem.at[sweep, d, 1 - side],
            device_id={AXES[d]: neighbour(d, side)},
            device_id_type=MESH,
        )

    sub = lax.broadcasted_iota(jnp.int32, (8, NK), 0)
    lane = lax.broadcasted_iota(jnp.int32, (8, NK), 1)
    lane_rev = NK - 1 - lane
    row_rev = 7 - sub
    row_swap = jnp.where(sub < 4, 3 - sub, sub)
    outer_k = jnp.logical_or(sub == 1, sub == 2)
    top_k = sub < 2
    last_k4 = jnp.logical_or(lane < 2, lane >= NK - 2)
    lane_rev_i = jnp.bitwise_xor(lane, CELLS - NJ)
    lane_rev_j = jnp.bitwise_xor(lane, NJ - 1)

    zero = jnp.zeros((2 * NJ, NK), jnp.float32)
    for v in range(FIELDS):
        u[v, pl.ds(0, 2 * NJ), :] = zero
        u[v, pl.ds(2 * NJ + CELLS, 2 * NJ), :] = zero
        gi[v, pl.ds(0, NJ), :] = zero[:NJ]
        gi[v, pl.ds(NJ + CELLS, NJ), :] = zero[:NJ]
    cross[...] = jnp.zeros((CELLS, NK), jnp.float32)

    def prepare():
        for load in load_rest[1:]:
            load.wait()
        high, low = halves(jnp.transpose(inv_k[...]))
        for h, part in enumerate((high, high, low)):
            w_k[pl.ds(h * NK, NK), :] = part
        def one_hot(index, shape):
            return jnp.where(index == lax.broadcasted_iota(jnp.int32, shape, 1), 1.0, 0.0).astype(
                jnp.float32
            )

        def taken(one, x):
            high, low = halves(x)
            return product(
                jnp.concatenate([one, one], axis=1).astype(BF16), jnp.concatenate([high, low], axis=0)
            )

        def pair(block_i, block_j):
            return taken(all_i, jnp.transpose(taken(block_i, t_i))) * taken(
                all_j, jnp.transpose(taken(block_j, t_j))
            )

        cell = lax.broadcasted_iota(jnp.int32, (CELLS, NI), 0)
        all_i = one_hot(lax.shift_right_logical(cell, 3), (CELLS, NI))
        cell = lax.broadcasted_iota(jnp.int32, (CELLS, NJ), 0)
        all_j = one_hot(jnp.bitwise_and(cell, 7), (CELLS, NJ))
        t_i = jnp.transpose(inv_i[...])
        t_j = jnp.transpose(inv_j[...])
        q = lax.broadcasted_iota(jnp.int32, (LATE, NI), 0)
        layer = lax.shift_right_logical(q, 3)
        edge = jnp.where(layer < 2, layer, NI + 1 - layer)
        late_i = one_hot(jnp.where(q < 4 * NJ, edge, jnp.bitwise_and(q, NI - 1)), (LATE, NI))
        q = lax.broadcasted_iota(jnp.int32, (LATE, NJ), 0)
        depth = jnp.where(q < 4 * NJ + NI, 0, 1)
        edge = far_side[1] * (NJ - 1) + (1 - 2 * far_side[1]) * depth
        late_j = one_hot(jnp.where(q < 4 * NJ, jnp.bitwise_and(q, 7), edge), (LATE, NJ))
        high, low = halves(pair(all_i, all_j))
        for h, part in enumerate((high, low, high)):
            m3[:, pl.ds(h * CELLS, CELLS)] = part
        high, low = halves(pair(late_i, late_j))
        late3[...] = jnp.concatenate([high, low, high], axis=1)

    prepare()
    load_rest[0].wait()
    load_u.wait()
    load_n.wait()

    def edge_i(sweep):
        for side in range(2):
            at = 0 if side == 0 else NI - 1
            back = 1 if side == 0 else NI - 2
            edge = [u[v, pl.ds((2 + at) * NJ, NJ), :] for v in range(FIELDS)]
            behind = [u[v, pl.ds((2 + back) * NJ, NJ), :] for v in range(FIELDS)]
            nn = [n[c, pl.ds(at * NJ, NJ), :] for c in range(3)]
            send, keep, far = face_terms(edge, behind, nn, -0.5 if side == 0 else 0.5)
            for v in range(FIELDS):
                send_i[sweep, side, v] = send[v]
                send_i[sweep, side, FIELDS + v] = far[v]
                keep_i[side, v] = keep[v]

    def edge_j(sweep):
        for side in range(2):
            at = 0 if side == 0 else NJ - 1
            back = 1 if side == 0 else NJ - 2
            edge = [u[v, pl.ds(2 * NJ + at, NI, stride=NJ), :] for v in range(FIELDS)]
            behind = [u[v, pl.ds(2 * NJ + back, NI, stride=NJ), :] for v in range(FIELDS)]
            nn = [n[3 + c, pl.ds(at, NI, stride=NJ), :] for c in range(3)]
            send, keep, far = face_terms(edge, behind, nn, -0.5 if side == 0 else 0.5)
            for v in range(FIELDS):
                send_j[sweep, side, v] = send[v]
                send_j[sweep, side, FIELDS + v] = far[v]
                keep_j[side, v] = keep[v]

    def edge_k(sweep):
        for i in range(NI):
            x = [u[v, pl.ds((2 + i) * NJ, NJ), :] for v in range(FIELDS)]
            if sweep == 0:
                x = x + [n[6 + c, pl.ds(i * NJ, NJ), :] for c in range(3)]
            y = pltpu.roll(x[0], 2, 1)
            for v in range(1, len(x)):
                y = jnp.where(lane >= 8 * v, pltpu.roll(x[v], 8 * v + 2, 1), y)
            cross[pl.ds(i * NJ, NJ), :] = y
        packed = jnp.transpose(cross[...])
        if sweep == 0:
            for c in range(3):
                n_k[c] = packed[8 * (FIELDS + c) : 8 * (FIELDS + c) + 8]
        edge = [packed[8 * v : 8 * v + 8] for v in range(FIELDS)]
        behind = [jnp.where(top_k, pltpu.roll(e, 1, 0), pltpu.roll(e, 7, 0)) for e in edge]
        half = jnp.where(top_k, 0.5, -0.5)
        send, keep, far = face_terms(edge, behind, [n_k[c] for c in range(3)], half)
        for v in range(FIELDS):
            next_rows = jnp.where(top_k, pltpu.roll(far[v], 7, 0), pltpu.roll(far[v], 1, 0))
            send_k[sweep, v] = rows(jnp.where(outer_k, send[v], next_rows), row_swap)
            keep_k[v] = jnp.where(outer_k, keep[v], next_rows)

    def interior():
        first_j, last_j = sub == 0, sub == NJ - 1
        first_k, last_k = lane == 0, lane == NK - 1

        def slab(i, carry):
            at = pl.multiple_of(i * NJ, NJ)
            g = [u[v, pl.ds(2 * NJ + at, NJ), :] for v in range(FIELDS)]
            nn = [n[c, pl.ds(at, NJ), :] for c in range(9)]
            inv, pressure = thermo(g)
            f = flux(g, inv, pressure, nn[0:3])
            for v in range(FIELDS):
                gi[v, pl.ds(NJ + at, NJ), :] = 0.5 * f[v]
            total = [-18.0 * damping * g[v] for v in range(FIELDS)]
            for d, axis, length, first, last in (
                (1, 0, NJ, first_j, last_j), (2, 1, NK, first_k, last_k),
            ):
                f = flux(g, inv, pressure, nn[3 * d : 3 * d + 3])
                for v in range(FIELDS):
                    def above(x):
                        return jnp.where(last, 0.0, pltpu.roll(x, length - 1, axis))

                    def below(x):
                        return jnp.where(first, 0.0, pltpu.roll(x, 1, axis))

                    smooth, half = 4.0 * damping * g[v], 0.5 * f[v]
                    up = smooth - half - damping * above(g[v])
                    down = smooth + half - damping * below(g[v])
                    total[v] = total[v] + above(up) + below(down)
            for v in range(FIELDS):
                r[v, pl.ds(at, NJ), :] = total[v]
            return carry

        lax.fori_loop(0, NI, slab, 0, unroll=4)

        def chord(i, carry):
            at = pl.multiple_of(i * NJ, NJ)
            for v in range(FIELDS):
                layer = [u[v, pl.ds(at + q * NJ, NJ), :] for q in (0, 1, 3, 4)]
                r[v, pl.ds(at, NJ), :] = (
                    r[v, pl.ds(at, NJ), :]
                    + gi[v, pl.ds(at, NJ), :]
                    - gi[v, pl.ds(at + 2 * NJ, NJ), :]
                    + 4.0 * damping * (layer[1] + layer[2])
                    - damping * (layer[0] + layer[3])
                )
            return carry

        lax.fori_loop(0, NI, chord, 0, unroll=4)

    def halo_k(sweep):
        for side in range(2):
            copy(sweep, 2, side).wait_recv()
        code = [jnp.full((8, NK), codes[0, q], jnp.int32) for q in range(4, 6)]
        flip_i = jnp.bitwise_and(jnp.where(top_k, code[1], code[0]) - 1, 1) == 1
        flip_j = jnp.bitwise_and(jnp.where(top_k, code[1], code[0]) - 1, 2) == 2
        linked = jnp.where(top_k, code[1], code[0]) > 0
        for v in range(FIELDS):
            z = jnp.where(top_k, recv_k[sweep, 1, v], recv_k[sweep, 0, v])
            z = jnp.where(flip_i, lanes(z, lane_rev_i), z)
            z = jnp.where(flip_j, lanes(z, lane_rev_j), z)
            cross[pl.ds(8 * v, 8), :] = jnp.where(linked, z, keep_k[v])
        spread = jnp.transpose(cross[...])
        for i in range(NI):
            part = pl.ds(i * NJ, NJ)
            x = spread[i * NJ : (i + 1) * NJ]
            for v in range(FIELDS):
                r[v, part, :] = r[v, part, :] + jnp.where(
                    last_k4, pltpu.roll(x, NK - 2 - 8 * v, 1), 0.0
                )

    def orientation(d, side):
        code = jnp.full((8, NK), codes[0, 2 * d + side], jnp.int32)
        first = jnp.bitwise_and(code - 1, 1) == 1
        second = jnp.bitwise_and(code - 1, 2) == 2
        return first, second, code > 0

    def halo_i(sweep, side):
        first, second, linked = orientation(0, side)
        for q in range(2 * FIELDS):
            v = q % FIELDS
            x = recv_i[sweep, side, q]
            x = jnp.where(first, rows(x, row_rev), x)
            x = jnp.where(second, lanes(x, lane_rev), x)
            own = keep_i[side, v] if q < FIELDS else send_i[sweep, side, q]
            x = jnp.where(linked, x, own)
            depth = 0 if q < FIELDS else 1
            at = pl.multiple_of((2 * side + depth) * NJ, NJ)
            late[v, pl.ds(at, NJ), :] = x

    def halo_j(sweep, side, far):
        if not far:
            copy(sweep, 1, 1 - side).wait_recv()
        first, second, linked = orientation(1, side)
        for q in range(2 * FIELDS):
            v = q % FIELDS
            x = [recv_j[sweep, side, q, pl.ds(8 * h, 8), :] for h in range(2)]
            rev = [rows(x[1 - h], row_rev) for h in range(2)]
            x = [jnp.where(first, rev[h], x[h]) for h in range(2)]
            x = [jnp.where(second, lanes(x[h], lane_rev), x[h]) for h in range(2)]
            depth = 0 if q < FIELDS else 1
            at = side * (NJ - 1) + (1 - 2 * side) * depth
            for h in range(2):
                part = pl.ds(8 * h, 8)
                own = keep_j[side, v, part, :] if q < FIELDS else send_j[sweep, side, q, part, :]
                y = jnp.where(linked, x[h], own)
                if far:
                    late[v, pl.ds(4 * NJ + depth * NI + 8 * h, 8), :] = y
                else:
                    where = pl.ds(8 * h * NJ + at, 8, stride=NJ)
                    r[v, where, :] = r[v, where, :] + y

    def add(sweep, v, change, first):
        if sweep == 0 and first:
            out[v] = change
        else:
            out[v] = out[v] + change
        if sweep == 0:
            inner = pl.ds(2 * NJ, CELLS)
            u[v, inner, :] = u[v, inner, :] + pseudo_step * change

    def solve_late(sweep):
        high, low = halves(late[...].reshape(FIELDS * LATE, NK))
        t = product(jnp.concatenate([high, low, high], axis=1), w_k[...])
        for group in ((0, 1, 2, 3), (4,)):
            high, low = halves(
                jnp.concatenate([t[v * LATE : (v + 1) * LATE] for v in group], axis=1)
            )
            both = product(late3[...], jnp.concatenate([high, high, low], axis=0))
            for q, v in enumerate(group):
                add(sweep, v, both[:, q * NK : (q + 1) * NK], False)

    def solve(sweep):
        for group in ((0, 1), (2, 3), (4,)):
            high, low = halves(jnp.concatenate([r[v] for v in group], axis=0))
            t = product(jnp.concatenate([high, low, high], axis=1), w_k[...])
            high, low = halves(
                jnp.concatenate([t[q * CELLS : (q + 1) * CELLS] for q in range(len(group))], axis=1)
            )
            both = product(m3[...], jnp.concatenate([high, high, low], axis=0))
            for q, v in enumerate(group):
                add(sweep, v, both[:, q * NK : (q + 1) * NK], True)

    for sweep in range(SWEEPS):
        edge_i(sweep)
        if sweep == 0:
            pl.semaphore_wait(barrier, 6)
        edge_j(sweep)
        copy(sweep, 1, far_side[1]).start()
        copy(sweep, 0, far_side[0]).start()
        edge_k(sweep)
        for side in range(2):
            copy(sweep, 2, side).start()
        copy(sweep, 0, 1 - far_side[0]).start()
        copy(sweep, 1, 1 - far_side[1]).start()
        interior()
        halo_j(sweep, 1 - far_side[1], False)
        halo_k(sweep)
        solve(sweep)
        copy(sweep, 0, 0).wait_recv()
        copy(sweep, 0, 1).wait_recv()
        copy(sweep, 1, 1 - far_side[1]).wait_recv()
        halo_i(sweep, 1 - far_side[0])
        halo_j(sweep, far_side[1], True)
        halo_i(sweep, far_side[0])
        solve_late(sweep)

    for sweep in range(SWEEPS):
        for d in range(3):
            for side in range(2):
                copy(sweep, d, side).wait_send()


def local(state, metrics, face_codes, inverse_i, inverse_j, inverse_k):
    f32 = jnp.float32
    vmem = pl.BlockSpec(memory_space=pltpu.VMEM)
    hbm = pl.BlockSpec(memory_space=pltpu.HBM)
    result = pl.pallas_call(
        kernel,
        out_shape=jax.ShapeDtypeStruct((FIELDS, CELLS, NK), f32),
        in_specs=[hbm] * 6,
        out_specs=vmem,
        scratch_shapes=[
            pltpu.SMEM((1, 6), jnp.int32),
            pltpu.VMEM((FIELDS, CELLS + 4 * NJ, NK), f32),
            pltpu.VMEM((9, CELLS, NK), f32),
            pltpu.VMEM((NI, NI), f32),
            pltpu.VMEM((NJ, NJ), f32),
            pltpu.VMEM((NK, NK), f32),
            pltpu.VMEM((FIELDS, CELLS, NK), f32),
            pltpu.VMEM((FIELDS, LATE, NK), f32),
            pltpu.VMEM((FIELDS, CELLS + 2 * NJ, NK), f32),
            pltpu.VMEM((3 * NK, NK), BF16),
            pltpu.VMEM((CELLS, 3 * CELLS), BF16),
            pltpu.VMEM((CELLS, 3 * LATE), BF16),
            pltpu.VMEM((CELLS, NK), f32),
            pltpu.VMEM((3, 8, NK), f32),
            pltpu.VMEM((SWEEPS, 2, 2 * FIELDS, NJ, NK), f32),
            pltpu.VMEM((SWEEPS, 2, 2 * FIELDS, NI, NK), f32),
            pltpu.VMEM((SWEEPS, FIELDS, 8, NK), f32),
            pltpu.VMEM((2, FIELDS, NJ, NK), f32),
            pltpu.VMEM((2, FIELDS, NI, NK), f32),
            pltpu.VMEM((FIELDS, 8, NK), f32),
            pltpu.VMEM((SWEEPS, 2, 2 * FIELDS, NJ, NK), f32),
            pltpu.VMEM((SWEEPS, 2, 2 * FIELDS, NI, NK), f32),
            pltpu.VMEM((SWEEPS, 2, FIELDS, 8, NK), f32),
            pltpu.SemaphoreType.DMA((6,)),
            pltpu.SemaphoreType.DMA((SWEEPS, 3, 2)),
            pltpu.SemaphoreType.DMA((SWEEPS, 3, 2)),
        ],
        compiler_params=pltpu.CompilerParams(
            collective_id=0, has_side_effects=True, vmem_limit_bytes=12 * 2**20
        ),
        name="adi",
    )(*(
        pltpu.with_memory_space_constraint(x, pltpu.HBM)
        for x in (
            face_codes.reshape(1, 6),
            state.reshape(FIELDS, CELLS, NK),
            metrics.reshape(9, CELLS, NK),
            inverse_i.reshape(NI, NI),
            inverse_j.reshape(NJ, NJ),
            inverse_k.reshape(NK, NK),
        )
    ))
    return result.reshape(state.shape)


def solution(mesh):
    cells = P(None, "chord", "normal", "span")
    block = P("chord", "normal", "span", None, None)
    return jax.shard_map(
        local,
        mesh=mesh,
        in_specs=(cells, cells, P("chord", "normal", "span", None), block, block, block),
        out_specs=cells,
        check_vma=False,
    )
```
